512 devices in a mesh: gx: 32 (over z, y_lo), gy: 16 (over x, y_hi, core).
Axes of the slice: x: 4, y: 8 (y_hi: 2, y_lo: 4; y = y_hi * 4 + y_lo), z: 8, core: 2. Of those that a mesh axis runs over, the one named last changes fastest.
Arguments:
- ensemble: float32 [40, 8, 64, 4096], P(None, None, 'gy', 'gx'), may hold values from 0.2 to 2
- courant_x: float32 [2, 64, 4096], P(None, 'gy', 'gx'), may hold values from -0.4 to 0.4
- courant_y: float32 [2, 64, 4096], P(None, 'gy', 'gx'), may hold values from -0.4 to 0.4
- diffusion: float32 [64, 4096], P('gy', 'gx'), may hold values from 0.02 to 0.12
- mixing: float32 [64, 4096], P('gy', 'gx'), may hold values from 0.02 to 0.2
- growth: float32 [2, 64, 4096], P(None, 'gy', 'gx'), may hold values from 0.05 to 0.5
- land_sea: int32 [64, 4096], P('gy', 'gx'), may hold values 0 or 1
- obs_cell: int32 [2, 1024], replicated, may hold values from 0 to 262143, as said below
- obs_value: float32 [2, 1024], replicated, may hold values from 0.2 to 2
- observation_variance: float32 [2, 1024], replicated, may hold values from 0.05 to 0.5
- obs_perturb: float32 [2, 1024, 40], replicated, may hold values from -4 to 4
- radius: int32 [1], replicated, may hold values from 32 to 64
Outputs:
- analysis: float32 [40, 8, 64, 4096], P(None, None, 'gy', 'gx')
The draws below stay inside these ranges and needn't reach their ends.
Inputs may be any that keep to these rules, and one draw needn't show every extreme that they name: obs_cell[b, k] is row * 4096 + column of the observed cell; with tiles of 4 rows and 128 columns, in each batch no tile holds more than 8 observed cells and some tile holds exactly 8.
All inputs are finite; a program needn't handle non-finite values. No bound on the sum of `land_sea` on one device may be relied on, other than what follows from the above.
Results may differ from the reference program's by a relative error of at most 0.0003.
Values sent between devices are 32-bit elements; how exact they have to be, the bound alone decides.
A program may use at most 64 MiB of HBM per device.

```python
import math
import jax
import jax.numpy as jnp
from jax import lax

MEMBERS = 40
LEVELS = 2
TRACER_COUNT = 4
FIELDS = 8
CX = 128
CY = 4
CAP = 8
BATCHES = 2
NOBS = 1024
NX = 4096
NY = 64


def observation_layout(key, batch_index):
    tiles_x = NX // CX
    tiles_y = NY // CY
    tile_count = tiles_x * tiles_y
    slot_count = tile_count * CAP
    sub_keys = jax.random.split(jax.random.fold_in(key, 101 + batch_index), 4)
    dense_tile = jax.random.randint(sub_keys[0], (), 0, tile_count)
    order_score = jax.random.permutation(sub_keys[1], slot_count).astype(jnp.int32)
    slot_ids = jnp.arange(slot_count, dtype=jnp.int32)
    order_score = jnp.where(slot_ids // CAP == dense_tile, slot_ids % CAP - CAP, order_score)
    chosen = jnp.argsort(order_score, stable=True)[:NOBS].astype(jnp.int32)
    chosen = chosen[jax.random.permutation(sub_keys[2], NOBS)]
    owner_tile = chosen // CAP
    local_cell = jax.random.randint(sub_keys[3], (NOBS,), 0, CX * CY)
    obs_row = owner_tile % tiles_y * CY + local_cell // CX
    obs_col = owner_tile // tiles_y * CX + local_cell % CX
    return (obs_row * NX + obs_col).astype(jnp.int32)


def draw_obs_cell(key, part):
    return jnp.stack([observation_layout(key, batch_index) for batch_index in range(BATCHES)])


def plant(array, stream_key, least, high):
    longest = array.shape.index(max(array.shape))
    spots = []
    for shift in (0, 1):
        where = [jax.random.randint(jax.random.fold_in(stream_key, axis), (), 0, length) for axis, length in enumerate(array.shape)]
        where[longest] = (where[longest] + shift) % array.shape[longest]
        spots.append(tuple(where))
    return array.at[spots[0]].set(least).at[spots[1]].set(high)


def shard_levels(own_key, dims, shards, low, largest):
    gain = 1.0
    for axis_at, parts in shards:
        steps = jax.random.uniform(jax.random.fold_in(jax.random.fold_in(own_key, 6), axis_at), (parts,), jnp.float32, low / len(shards), largest / len(shards))
        gain = gain * jnp.repeat(jnp.exp(steps), dims[axis_at] // parts).reshape((-1,) + (1,) * (len(dims) - 1 - axis_at))
    return gain


def gaussian(stream_key, shape, scale, reach, kind=jnp.bfloat16):
    array = scale * jax.random.normal(stream_key, shape, jnp.float32)
    return jnp.clip(array, min=-reach, max=reach).astype(kind)


def setup_inputs(seed: int = 0) -> dict:
    key_of = jax.random.split(jax.random.key(seed), 13)
    ensemble = jnp.clip(0.2 + 1.8 * jax.random.uniform(key_of[0], (MEMBERS, FIELDS, NY, NX), jnp.float32) ** shard_levels(key_of[0], (MEMBERS, FIELDS, NY, NX), ((2, 16), (3, 32)), -0.2, 0.2), 0.2, 2.0)
    courant_x = jnp.clip(jax.random.uniform(key_of[1], (LEVELS, NY, NX), jnp.float32, -0.4, 0.4) * shard_levels(key_of[1], (LEVELS, NY, NX), ((1, 16), (2, 32)), -0.4, 0.0), -0.4, 0.4)
    courant_y = jnp.clip(jax.random.uniform(key_of[2], (LEVELS, NY, NX), jnp.float32, -0.4, 0.4) * shard_levels(key_of[2], (LEVELS, NY, NX), ((1, 16), (2, 32)), -0.4, 0.0), -0.4, 0.4)
    diffusion = jnp.clip(jnp.exp(math.log(0.12) - 1.7917595 * jax.random.uniform(key_of[3], (NY, NX), jnp.float32) ** shard_levels(key_of[3], (NY, NX), ((0, 16), (1, 32)), -0.2, 0.2)), 0.02, 0.12)
    mixing = jnp.clip(jnp.exp(math.log(0.2) - 2.3025851 * jax.random.uniform(key_of[4], (NY, NX), jnp.float32) ** shard_levels(key_of[4], (NY, NX), ((0, 16), (1, 32)), -0.2, 0.2)), 0.02, 0.2)
    growth = jnp.clip(jnp.exp(math.log(0.5) - 2.3025851 * jax.random.uniform(key_of[5], (LEVELS, NY, NX), jnp.float32) ** shard_levels(key_of[5], (LEVELS, NY, NX), ((1, 16), (2, 32)), -0.2, 0.2)), 0.05, 0.5)
    land_sea = plant((jax.random.randint(key_of[6], (NY, NX), 0, 4) < 3).astype(jnp.int32), jax.random.fold_in(key_of[6], 1), 0, 1)
    obs_cell = draw_obs_cell(jax.random.fold_in(key_of[12], 71), 0)
    obs_value = jnp.clip(jax.random.uniform(key_of[8], (BATCHES, NOBS), jnp.float32, 0.2, 2.0), 0.2, 2.0)
    observation_variance = jnp.clip(jnp.exp(jax.random.uniform(key_of[9], (BATCHES, NOBS), jnp.float32, math.log(0.05), math.log(0.5))), 0.05, 0.5)
    obs_perturb = gaussian(key_of[10], (BATCHES, NOBS, MEMBERS), 1.0, 4.0, jnp.float32)
    radius = jax.random.randint(key_of[11], (1,), NY // 2, CX // 2 + 1).astype(jnp.int32)
    return dict(ensemble=ensemble, courant_x=courant_x, courant_y=courant_y, diffusion=diffusion, mixing=mixing, growth=growth, land_sea=land_sea, obs_cell=obs_cell, obs_value=obs_value, observation_variance=observation_variance, obs_perturb=obs_perturb, radius=radius)


def upwind(minus_two, minus_one, center, plus_one, plus_two, courant):
    rising = (2.0 * plus_one + 3.0 * center - 6.0 * minus_one + minus_two) / 6.0
    falling = (-plus_two + 6.0 * plus_one - 3.0 * center - 2.0 * minus_one) / 6.0
    return -(jnp.maximum(courant, 0.0) * rising + jnp.minimum(courant, 0.0) * falling)

def transport(padded, courant_x, courant_y, diffusion):
    row_count = padded.shape[-2] - 4
    columns = padded.shape[-1] - 4

    def offset(row_shift, col_shift):
        return padded[..., 2 + row_shift:2 + row_shift + row_count, 2 + col_shift:2 + col_shift + columns]
    center = offset(0, 0)
    along_x = upwind(offset(0, -2), offset(0, -1), center, offset(0, 1), offset(0, 2), courant_x[:, None])
    along_y = upwind(offset(-2, 0), offset(-1, 0), center, offset(1, 0), offset(2, 0), courant_y[:, None])
    spread = offset(0, 1) + offset(0, -1) + offset(1, 0) + offset(-1, 0) - 4.0 * center
    return (center, along_x + along_y + diffusion * spread)

def tendency(fields, growth, mixing):
    nutrient = fields[..., 0, :, :]
    plankton = fields[..., 1, :, :]
    grazer = fields[..., 2, :, :]
    detritus = fields[..., 3, :, :]
    uptake = growth * jnp.abs(nutrient) / (jnp.abs(nutrient) + 0.5) * plankton
    grazing = 0.3 * grazer * jnp.abs(plankton) / (jnp.abs(plankton) + 0.5)
    biology = jnp.stack([-uptake + 0.1 * detritus, uptake - grazing - 0.05 * plankton, 0.3 * grazing - 0.05 * grazer, 0.7 * grazing + 0.05 * plankton + 0.05 * grazer - 0.1 * detritus], axis=-3)
    upper_level = fields[..., 0, :, :, :]
    lower_level = fields[..., 1, :, :, :]
    vertical = jnp.stack([mixing * (lower_level - upper_level), mixing * (upper_level - lower_level)], axis=-4)
    return biology + vertical

def assimilate(present_state, cells, values, variances, perturbs, radius_sq, ocean_mask):
    obs_rows = cells // NX
    obs_cols = cells % NX
    prior_slots = present_state[:, 1][:, obs_rows, obs_cols].T
    anomaly = prior_slots - lax.optimization_barrier(jnp.mean(prior_slots, axis=1, keepdims=True))
    spread_var = lax.optimization_barrier(jnp.sum(anomaly * anomaly, axis=1)) / (MEMBERS - 1)
    obs_scale = 1.0 / ((MEMBERS - 1) * (spread_var + variances))
    innovation = values[:, None] + jnp.sqrt(variances)[:, None] * perturbs - prior_slots
    member_deviation = present_state - lax.optimization_barrier(jnp.mean(present_state, axis=0, keepdims=True))
    half_width = CX // 2
    width_win = 2 * half_width + 1
    padded = jnp.concatenate([member_deviation[..., NX - half_width:], member_deviation, member_deviation[..., :half_width]], axis=3)
    row_index = jnp.arange(NY, dtype=jnp.int32)
    window_cols = (jnp.arange(width_win, dtype=jnp.int32) - half_width).astype(jnp.float32)

    def one_obs(accumulated, packed):
        row_obs, col_obs, anom_row, innov_row, scale_obs = packed
        window = lax.dynamic_slice_in_dim(padded, col_obs, width_win, 3)
        covariance = jnp.einsum('mfyx,m->fyx', window, anom_row, precision=lax.Precision.HIGHEST)
        row_gap = (row_obs - row_index).astype(jnp.float32)
        distance = row_gap[:, None] * row_gap[:, None] + window_cols[None, :] * window_cols[None, :]
        taper_weight = jnp.maximum(0.0, 1.0 - distance / radius_sq)
        gain_block = covariance * taper_weight * scale_obs
        existing = lax.dynamic_slice_in_dim(accumulated, col_obs, width_win, 3)
        update = existing + jnp.einsum('fyx,m->mfyx', gain_block, innov_row, precision=lax.Precision.HIGHEST)
        return (lax.dynamic_update_slice_in_dim(accumulated, update, col_obs, 3), None)
    start = jnp.zeros((MEMBERS, FIELDS, NY, NX + 2 * half_width), jnp.float32)
    accumulated, _ = lax.scan(one_obs, start, (obs_rows, obs_cols, anomaly, innovation, obs_scale))
    increment = accumulated[..., half_width:half_width + NX]
    increment = increment.at[..., :half_width].add(accumulated[..., NX + half_width:])
    increment = increment.at[..., NX - half_width:].add(accumulated[..., :half_width])
    return present_state + ocean_mask * increment

def reference(ensemble, courant_x, courant_y, diffusion, mixing, growth, land_sea, obs_cell, obs_value, observation_variance, obs_perturb, radius):
    ocean_mask = land_sea.astype(jnp.float32)

    def predicted_member(ensemble_member):
        fields = ensemble_member.reshape(LEVELS, TRACER_COUNT, NY, NX)
        widened = jnp.concatenate([fields[..., NX - 2:], fields, fields[..., :2]], axis=3)
        padded = jnp.pad(widened, ((0, 0), (0, 0), (2, 2), (0, 0)))
        center, carried = transport(padded, courant_x, courant_y, diffusion)
        result = center + ocean_mask * (carried + tendency(center, growth, mixing))
        return result.reshape(FIELDS, NY, NX)
    present_state = lax.map(predicted_member, ensemble)
    radius_sq = radius[0].astype(jnp.float32) * radius[0].astype(jnp.float32)
    for batch_index in range(BATCHES):
        present_state = assimilate(present_state, obs_cell[batch_index], obs_value[batch_index], observation_variance[batch_index], obs_perturb[batch_index], radius_sq, ocean_mask)
    return present_state
```

```python
import functools

import jax
import jax.numpy as jnp
from jax import lax
from jax.experimental import pallas as pl
from jax.experimental.pallas import tpu as pltpu
from jax.sharding import PartitionSpec as P

MESH = pl.DeviceIdType.MESH
F32 = jnp.float32
BF16 = jnp.bfloat16
M = 40
FIELDS = 8
ROWS = 4
COLS = 128
TX = 32
TY = 16
NX = 4096
NOBS = 1024
CAP = 8
SLOTS = 3 * TY * CAP
CHUNKS = NOBS // 128
BLOCK = 128
ORDER = (1, 0, 2, 3, 4, 5, 6, 7)
PARTNERS = [
    (dc, dj) for dj in (4, 3, 5, 2, 6, 1, 7, 0) for dc in (1, -1, 0) if (dc, dj) != (0, 0)
]


def dot(a, b):
    return lax.dot_general(a, b, (((1,), (0,)), ((), ())), preferred_element_type=F32)


def dot_t(a, b):
    return lax.dot_general(a, b, (((1,), (1,)), ((), ())), preferred_element_type=F32)


def split3(x):
    high = x.astype(BF16)
    rest = x - high.astype(F32)
    mid = rest.astype(BF16)
    low = (rest - mid.astype(F32)).astype(BF16)
    return high, mid, low


def iota(shape, dim):
    return lax.broadcasted_iota(jnp.int32, shape, dim)


def forecast_kernel(
    ens_ref,
    cx_ref,
    cy_ref,
    diff_ref,
    mix_ref,
    growth_ref,
    land_ref,
    cell_ref,
    value_ref,
    var_ref,
    pert_ref,
    radius_ref,
    x_ref,
    slots_ref,
    tab_ref,
    row_ref,
    count_ref,
    y_ref,
    halo_ref,
    edge_ref,
    side_ref,
    rec_ref,
    got_ref,
    cell_s,
    rank_s,
    trans_s,
    v_ref,
    hot_ref,
    coef_ref,
    load_sem,
    halo_send,
    halo_recv,
    edge_send,
    edge_recv,
    rec_send,
    rec_recv,
    swap_send,
    swap_recv,
):
    gx = lax.axis_index("gx")
    gy = lax.axis_index("gy")
    core = lax.rem(gy, 2)
    above = (gx, lax.rem(gy + TY - 1, TY))
    below = (gx, lax.rem(gy + 1, TY))
    left = (lax.rem(gx + TX - 1, TX), gy)
    right = (lax.rem(gx + 1, TX), gy)
    sibling = (gx, gy + 1 - 2 * core)

    def partner(dc, dj):
        return (lax.rem(gx + dc + TX, TX), lax.rem(gy + 2 * dj, TY))

    barrier = pltpu.get_barrier_semaphore()
    for device in [partner(dc, dj) for dc, dj in PARTNERS] + [above, below]:
        pl.semaphore_signal(barrier, inc=1, device_id=device, device_id_type=MESH)

    loads = []
    for f in ORDER:
        for r in range(ROWS):
            copy = pltpu.make_async_copy(
                ens_ref.at[:, f * ROWS + r, 0, :], y_ref.at[f, r], load_sem.at[f, r]
            )
            copy.start()
            loads.append(copy)

    col_start = gx * COLS
    row_start = gy * ROWS
    me = gx * TY + gy
    sub = iota((8, 128), 0)
    lane = iota((8, 128), 1)
    big_sub = iota((128, 128), 0)
    big_lane = iota((128, 128), 1)
    own_hot = []
    places = []
    for b in range(2):
        for j in range(CHUNKS):
            cell_s[b, j : j + 1, :] = cell_ref[b : b + 1, 128 * j : 128 * j + 128]
        cell = cell_s[b]
        row = cell >> 12
        col = cell & (NX - 1)
        tile_col = col >> 7
        owner = (tile_col * TY + (row >> 2)).astype(F32)
        for i in range(CHUNKS):
            trans_s[i] = jnp.broadcast_to(owner[i : i + 1, :], (128, 128)).T
        for j in range(CHUNKS):
            mine = jnp.broadcast_to(owner[j : j + 1, :], (128, 128))
            total = jnp.where((trans_s[j] == mine) & (big_sub < big_lane), 1.0, 0.0)
            for i in range(j):
                total = total + jnp.where(trans_s[i] == mine, 1.0, 0.0)
            rank_s[b, j : j + 1, :] = jnp.sum(total, axis=0, keepdims=True)
        rank = rank_s[b]
        own_slot = jnp.where(owner == me.astype(F32), rank, -1.0)
        local_cell = ((row - row_start) * COLS + (col - col_start)).astype(F32)
        subf = sub.astype(F32)
        spot = jnp.zeros((8, 128), F32)
        fill = jnp.zeros((8, 128), F32)
        for j in range(CHUNKS):
            hit = subf == own_slot[j : j + 1, :]
            spot = spot + jnp.where(hit, local_cell[j : j + 1, :], 0.0)
            fill = fill + jnp.where(hit, 1.0, 0.0)
        spot = jnp.sum(spot, axis=1, keepdims=True)
        fill = jnp.sum(fill, axis=1, keepdims=True)
        lane512 = iota((8, ROWS * COLS), 1).astype(F32)
        own_hot.append(jnp.where((spot == lane512) & (fill > 0.0), 1.0, 0.0))
        places.append((row, col, tile_col, rank))
    own_hot = jnp.concatenate(own_hot, axis=0).astype(BF16)

    ocean = land_ref[...].astype(F32)
    first = gy == 0
    last = gy == TY - 1
    for level in range(2):
        for r in range(ROWS):
            at = level * ROWS + r
            o = ocean[r : r + 1, :]
            d = diff_ref[r : r + 1, :] * o
            cx = cx_ref[at : at + 1, :] * o
            cy = cy_ref[at : at + 1, :] * o
            xp, xn = jnp.maximum(cx, 0.0), jnp.minimum(cx, 0.0)
            yp, yn = jnp.maximum(cy, 0.0), jnp.minimum(cy, 0.0)
            terms = [
                1.0 + 0.5 * (xn - xp + yn - yp) - 4.0 * d,
                xn / 6.0,
                d - xp / 3.0 - xn,
                d + xp + xn / 3.0,
                -xp / 6.0,
                yn / 6.0,
                d - yp / 3.0 - yn,
                d + yp + yn / 3.0,
                -yp / 6.0,
            ]
            if r == 0:
                terms[7] = jnp.where(first, 0.0, terms[7])
            if r <= 1:
                terms[8] = jnp.where(first, 0.0, terms[8])
            if r == 3:
                terms[6] = jnp.where(last, 0.0, terms[6])
            if r >= 2:
                terms[5] = jnp.where(last, 0.0, terms[5])
            for i, term in enumerate(terms):
                coef_ref[at, i] = jnp.broadcast_to(term, (8, 128))
            coef_ref[at, 9] = jnp.broadcast_to(o * mix_ref[r : r + 1, :], (8, 128))
            coef_ref[at, 10] = jnp.broadcast_to(o, (8, 128))
            coef_ref[at, 11] = jnp.broadcast_to(growth_ref[at : at + 1, :], (8, 128))

    for n, f in enumerate(ORDER):
        for r in range(ROWS):
            loads[n * ROWS + r].wait()
        packed = jnp.zeros((8, 128), F32)
        for r in range(ROWS):
            for i in range(M // 8):
                at = 4 * (r * (M // 8) + i)
                moved = pltpu.roll(y_ref[f, r, 8 * i : 8 * i + 8, :], (at + 2) % 128, 1)
                packed = jnp.where((lane >= at) & (lane < at + 4), moved, packed)
        edge_ref[n] = packed

    pl.semaphore_wait(barrier, len(PARTNERS) + 2)

    halos = {}

    def send_rows(f):
        for side, (device, start) in enumerate(((below, 2), (above, 0))):
            copy = pltpu.make_async_remote_copy(
                src_ref=y_ref.at[f, pl.ds(start, 2)],
                dst_ref=halo_ref.at[f, side],
                send_sem=halo_send.at[f, side],
                recv_sem=halo_recv.at[f, side],
                device_id=device,
                device_id_type=MESH,
            )
            copy.start()
            halos[f, side] = copy

    edges = {}

    def send_edges(part, window):
        for side, device in enumerate((right, left)):
            copy = pltpu.make_async_remote_copy(
                src_ref=edge_ref.at[window],
                dst_ref=side_ref.at[side, window],
                send_sem=edge_send.at[part, side],
                recv_sem=edge_recv.at[part, side],
                device_id=device,
                device_id_type=MESH,
            )
            copy.start()
            edges[part, side] = copy

    send_rows(ORDER[0])
    send_edges(0, pl.ds(0, 1))
    send_edges(1, pl.ds(1, FIELDS - 1))
    for f in ORDER[1:]:
        send_rows(f)

    def by_member(value, r, at):
        return jnp.broadcast_to(coef_ref[at, value][None], (M // 8, 8, 128)).reshape(M, 128)

    wide_lane = iota((M, 128), 1)

    def inner(n, f):
        level, tracer = divmod(f, 4)
        base = level * 4
        merged = jnp.where((lane & 3) < 2, side_ref[0, n], side_ref[1, n])
        for r in range(ROWS):
            at = level * ROWS + r
            c = functools.partial(by_member, r=r, at=at)
            q = y_ref[f, r]
            halo = jnp.concatenate(
                [
                    pltpu.roll(merged, (126 - 4 * (r * (M // 8) + i)) % 128, 1)
                    for i in range(M // 8)
                ],
                axis=0,
            )
            total = q * c(0)
            total += c(1) * pltpu.roll(jnp.where(wide_lane < 2, halo, q), 126, 1)
            total += c(2) * pltpu.roll(jnp.where(wide_lane < 1, halo, q), 127, 1)
            total += c(3) * pltpu.roll(jnp.where(wide_lane > 126, halo, q), 1, 1)
            total += c(4) * pltpu.roll(jnp.where(wide_lane > 125, halo, q), 2, 1)
            for value, shift in ((5, 2), (6, 1), (7, -1), (8, -2)):
                if 0 <= r + shift < ROWS:
                    total += c(value) * y_ref[f, r + shift]
            total += c(9) * (y_ref[(1 - level) * 4 + tracer, r] - q)
            plankton = y_ref[base + 1, r]
            grazer = y_ref[base + 2, r]
            uptake = grazing = 0.0
            if tracer in (0, 1):
                nutrient = jnp.abs(y_ref[base, r])
                uptake = c(11) * nutrient / (nutrient + 0.5) * plankton
            if tracer in (1, 2, 3):
                size = jnp.abs(plankton)
                grazing = 0.3 * grazer * size / (size + 0.5)
            if tracer == 0:
                change = 0.1 * y_ref[base + 3, r] - uptake
            elif tracer == 1:
                change = uptake - grazing - 0.05 * plankton
            elif tracer == 2:
                change = 0.3 * grazing - 0.05 * grazer
            else:
                change = 0.7 * grazing + 0.05 * plankton + 0.05 * grazer - 0.1 * q
            x_ref[f * ROWS + r] = total + c(10) * change

    def outer(f):
        at = f // 4 * ROWS
        far, near = halo_ref[f, 0, 0], halo_ref[f, 0, 1]
        x_ref[f * ROWS] += by_member(8, 0, at) * far + by_member(7, 0, at) * near
        x_ref[f * ROWS + 1] += by_member(8, 1, at + 1) * near
        near, far = halo_ref[f, 1, 0], halo_ref[f, 1, 1]
        x_ref[f * ROWS + 2] += by_member(5, 2, at + 2) * near
        x_ref[f * ROWS + 3] += by_member(5, 3, at + 3) * far + by_member(6, 3, at + 3) * near

    f = ORDER[0]
    for side in range(2):
        edges[0, side].wait_recv()
    inner(0, f)
    for side in range(2):
        halos[f, side].wait_recv()
    outer(f)

    fields = jnp.concatenate(
        [
            jnp.concatenate(
                [x_ref[f * ROWS + r], jnp.broadcast_to(ocean[r : r + 1, :], (8, 128))], axis=0
            )
            for r in range(ROWS)
        ],
        axis=1,
    )
    high, mid, low = split3(fields)
    prior = dot_t(own_hot, high) + dot_t(own_hot, mid) + dot_t(own_hot, low)
    rec_ref[...] = jnp.zeros((8, 128), F32)
    rec_ref[:, 0:48] = prior[0:8]
    rec_ref[:, 64:112] = prior[8:16]
    half = gy // 2
    got_ref[1, half, core] = rec_ref[...]
    records = []
    for i, (dc, dj) in enumerate(PARTNERS):
        copy = pltpu.make_async_remote_copy(
            src_ref=rec_ref,
            dst_ref=got_ref.at[1 - dc, half, core],
            send_sem=rec_send.at[i],
            recv_sem=rec_recv.at[i],
            device_id=partner(dc, dj),
            device_id_type=MESH,
        )
        copy.start()
        records.append(copy)

    reach = radius_ref[0] * radius_ref[0]
    upper = jnp.where(big_sub < big_lane, 1.0, 0.0).astype(BF16)

    def before(flag):
        flag = jnp.where(flag, 1.0, 0.0)
        inside = dot(flag.astype(BF16), upper)
        own = jnp.broadcast_to(jnp.sum(flag, axis=1, keepdims=True), (8, 128))
        run = own
        for step in (1, 2, 4):
            run = run + jnp.where(sub >= step, pltpu.roll(run, step, 0), 0.0)
        return inside + run - own, run[7:8, :]

    count_ref[...] = jnp.zeros((8, 128), F32)
    for b in range(2):
        row, col, tile_col, rank = places[b]
        relative = (tile_col - gx + 33) & (TX - 1)
        slot = ((relative * TY + (row >> 2)) * CAP).astype(F32) + rank
        offset = ((col - (col_start + 64) + 2048 + NX) & (NX - 1)) - 2048
        gap_x = jnp.maximum(0, jnp.maximum(offset - 63, -64 - offset))
        gap_y = jnp.maximum(0, jnp.maximum(row - (row_start + 3), row_start - row))
        gap = gap_x * gap_x + gap_y * gap_y
        near = gap < reach
        place, count = before(near)
        place = jnp.where(near, place, -1.0)
        count_ref[2 * b : 2 * b + 1, :] = count
        if b == 0:
            beyond = (gap >= reach) & (gap < 4 * reach)
            place2, count2 = before(beyond)
            place = jnp.where(beyond, place2 + count, place)
            count_ref[1:2, :] = count + count2
        v_ref[0:1, :] = value_ref[b : b + 1, :]
        v_ref[1:2, :] = var_ref[b : b + 1, :]
        rowf, colf = row.astype(F32), col.astype(F32)
        for j in range(CHUNKS):
            window = slice(128 * j, 128 * j + 128)
            v_ref[2:3, window] = rowf[j : j + 1, :]
            v_ref[3:4, window] = colf[j : j + 1, :]
            v_ref[4:5, window] = slot[j : j + 1, :]
        v_ref[5:8, :] = jnp.ones((3, NOBS), F32)
        index = iota((SLOTS, 128), 0).astype(F32)
        for j in range(CHUNKS):
            hot = jnp.where(index == place[j : j + 1, :], 1.0, 0.0)
            hot_ref[:, 128 * j : 128 * j + 128] = hot.astype(BF16)
        hot = hot_ref[...]
        vs = split3(v_ref[...])
        column = dot_t(hot, vs[0]) + dot_t(hot, vs[1]) + dot_t(hot, vs[2])
        row_ref[b] = dot_t(vs[0], hot) + dot_t(vs[1], hot) + dot_t(vs[2], hot)
        ps = split3(pert_ref[b])
        noise = dot(hot, ps[0]) + dot(hot, ps[1]) + dot(hot, ps[2])
        tab_ref[b] = jnp.zeros((SLOTS, 128), F32)
        tab_ref[b, :, 0:M] = column[:, 0:1] + jnp.sqrt(column[:, 1:2]) * noise
        tab_ref[b, :, M : M + 8] = column

    for side in range(2):
        edges[1, side].wait_recv()
    for n, f in enumerate(ORDER):
        if n:
            inner(n, f)
    for copy in records:
        copy.wait_recv()
    swap = pltpu.make_async_remote_copy(
        src_ref=got_ref.at[:, :, core],
        dst_ref=got_ref.at[:, :, core],
        send_sem=swap_send,
        recv_sem=swap_recv,
        device_id=sibling,
        device_id_type=MESH,
    )
    swap.start()
    for f in ORDER[1:]:
        for side in range(2):
            halos[f, side].wait_recv()
        outer(f)
    swap.wait_recv()
    slots_ref[...] = got_ref[...].reshape(SLOTS, 128)
    swap.wait_send()
    for copy in records:
        copy.wait_send()
    for f in ORDER:
        for side in range(2):
            halos[f, side].wait_send()
    for part in range(2):
        for side in range(2):
            edges[part, side].wait_send()


def analysis_kernel(
    x_ref,
    slots_ref,
    tab_ref,
    row_ref,
    count_ref,
    land_ref,
    radius_ref,
    out_ref,
    state_ref,
    part_ref,
    anom_ref,
    scaled_ref,
    innov_ref,
    lhs_ref,
    rhs_ref,
    weight_ref,
    dev_ref,
    out_sem,
):
    gx = lax.axis_index("gx")
    gy = lax.axis_index("gy")
    radius = radius_ref[0].astype(F32)
    per_square = 1.0 / jnp.full((1, 128), radius * radius, F32)
    lane = iota((BLOCK, 128), 1)
    member = lane < M
    counts = [jnp.max(count_ref[i : i + 1, :]).astype(jnp.int32) for i in range(3)]
    blocks0, blocks0_wide, blocks1 = [(n + BLOCK - 1) // BLOCK for n in counts]
    for i, piece in enumerate(split3(slots_ref[...])):
        part_ref[i] = piece
    ocean = land_ref[...].astype(F32)
    exact = functools.partial(
        lax.dot_general, precision=lax.Precision.HIGHEST, preferred_element_type=F32
    )

    def near_x(gap):
        gap = jnp.where(gap >= NX / 2, gap - NX, gap)
        return jnp.where(gap < -NX / 2, gap + NX, gap)

    def load(b, j):
        start = pl.multiple_of(j * BLOCK, BLOCK)
        tab = tab_ref[b, pl.ds(start, BLOCK), :]
        slot = tab[:, M + 4 : M + 5]
        hot = jnp.where(iota((BLOCK, SLOTS), 1).astype(F32) == slot, 1.0, 0.0).astype(BF16)
        prior = dot(hot, part_ref[0]) + dot(hot, part_ref[1]) + dot(hot, part_ref[2])
        if b:
            prior = pltpu.roll(prior, 64, 1)
        return tab, prior

    def finish(b, j, tab, prior):
        prior = jnp.where(member, prior, 0.0)
        anomaly = jnp.where(
            member, prior - jnp.sum(prior, axis=1, keepdims=True) * (1.0 / M), 0.0
        )
        spread = jnp.sum(anomaly * anomaly, axis=1, keepdims=True) * (1.0 / (M - 1))
        filled = tab[:, M + 5 : M + 6]
        scale = filled / ((M - 1) * (spread + tab[:, M + 1 : M + 2] + (1.0 - filled)))
        innovation = jnp.where(member, tab, 0.0) - prior
        if b == 0:
            scaled_ref[j] = anomaly * scale
            innov_ref[j] = innovation
        high = anomaly.astype(BF16).astype(F32)
        lhs = high + pltpu.roll(high, M, 1) + pltpu.roll(anomaly - high, 2 * M, 1)
        anom_ref[b, j] = lhs.astype(BF16)
        turned = innovation.T[0:M, :]
        high = turned.astype(BF16).astype(F32)
        lhs = jnp.concatenate(
            [
                jnp.concatenate([high, high], axis=1),
                jnp.concatenate([turned - high, jnp.zeros_like(high)], axis=1),
            ],
            axis=0,
        )
        lhs_ref[b, j] = lhs.astype(BF16)
        gap = near_x(tab[:, M + 3 : M + 4] - (gx * COLS + lane).astype(F32))
        square = gap * gap
        for r in range(ROWS):
            gap = tab[:, M + 2 : M + 3] - (gy * ROWS + r).astype(F32)
            taper = jnp.maximum(0.0, 1.0 - (square + gap * gap) * per_square)
            weight_ref[b, j, :, 128 * r : 128 * r + 128] = taper * scale

    def first_batch(j, carry):
        tab, prior = load(0, j)
        finish(0, j, tab, prior)
        return carry

    first_batch(0, 0)
    lax.fori_loop(1, blocks0_wide, first_batch, 0)

    def second_batch(j, carry):
        tab, prior = load(1, j)
        wet = prior[:, M : M + 1]
        inside = jnp.where(member, prior, 0.0)
        deviation = jnp.where(
            member, inside - jnp.sum(inside, axis=1, keepdims=True) * (1.0 / M), 0.0
        )

        def add(i, total):
            cover = exact(deviation, scaled_ref[i], (((1,), (1,)), ((), ())))
            window = pl.ds(pl.multiple_of(i * BLOCK, BLOCK), BLOCK)
            gap_x = near_x(row_ref[0, 3:4, window] - tab[:, M + 3 : M + 4])
            gap_y = row_ref[0, 2:3, window] - tab[:, M + 2 : M + 3]
            taper = jnp.maximum(0.0, 1.0 - (gap_x * gap_x + gap_y * gap_y) * per_square)
            return total + exact(cover * taper, innov_ref[i], (((1,), (0,)), ((), ())))

        total = lax.fori_loop(1, blocks0_wide, add, add(0, jnp.zeros((BLOCK, 128), F32)))
        finish(1, j, tab, inside + wet * total)
        return carry

    second_batch(0, 0)
    lax.fori_loop(1, blocks1, second_batch, 0)

    def spread_field(source, f):
        for r in range(ROWS):
            x = source[f * ROWS + r]
            deviation = x - jnp.sum(x, axis=0, keepdims=True) * (1.0 / M)
            high = deviation.astype(BF16).astype(F32)
            stack = jnp.concatenate(
                [high, deviation - high, high, jnp.zeros((8, 128), F32)], axis=0
            )
            dev_ref[f, :, 128 * r : 128 * r + 128] = stack.astype(BF16)

    def increment(b, j, f):
        cover = dot(anom_ref[b, j], dev_ref[f])
        gain = cover * weight_ref[b, j]
        high = gain.astype(BF16)
        low = (gain - high.astype(F32)).astype(BF16)
        both = dot(lhs_ref[b, j], jnp.concatenate([high, low], axis=0))
        return both[0:M] + both[M : 2 * M]

    def apply(b, blocks, source):
        def field(f, carry):
            spread_field(source, f)
            change = increment(b, 0, f)
            for r in range(ROWS):
                state_ref[f * ROWS + r] = (
                    source[f * ROWS + r] + ocean[r : r + 1, :] * change[:, 128 * r : 128 * r + 128]
                )
            return carry

        lax.fori_loop(0, FIELDS, field, 0, unroll=2)

        def more(j, carry):
            def field_more(f, inner_carry):
                change = increment(b, j, f)
                for r in range(ROWS):
                    state_ref[f * ROWS + r] += (
                        ocean[r : r + 1, :] * change[:, 128 * r : 128 * r + 128]
                    )
                return inner_carry

            return lax.fori_loop(0, FIELDS, field_more, carry)

        lax.fori_loop(1, blocks, more, 0)

    apply(0, blocks0, x_ref)
    apply(1, blocks1, state_ref)
    copies = []
    for i in range(FIELDS * ROWS):
        copy = pltpu.make_async_copy(
            state_ref.at[i], out_ref.at[:, i, 0, :], out_sem.at[i]
        )
        copy.start()
        copies.append(copy)
    for copy in copies:
        copy.wait()


def local(
    ensemble,
    courant_x,
    courant_y,
    diffusion,
    mixing,
    growth,
    land_sea,
    obs_cell,
    obs_value,
    observation_variance,
    obs_perturb,
    radius,
):
    vmem = pl.BlockSpec(memory_space=pltpu.VMEM)
    smem = pl.BlockSpec(memory_space=pltpu.SMEM)
    hbm = pl.BlockSpec(memory_space=pl.ANY)
    shape = jax.ShapeDtypeStruct
    dma = pltpu.SemaphoreType.DMA
    x, slots, tab, rows, count = pl.pallas_call(
        forecast_kernel,
        out_shape=(
            shape((FIELDS * ROWS, M, COLS), F32),
            shape((SLOTS, 128), F32),
            shape((2, SLOTS, 128), F32),
            shape((2, 8, SLOTS), F32),
            shape((8, 128), F32),
        ),
        in_specs=[hbm] + [vmem] * 10 + [smem],
        out_specs=(vmem,) * 5,
        scratch_shapes=[
            pltpu.VMEM((FIELDS, ROWS, M, COLS), F32),
            pltpu.VMEM((FIELDS, 2, 2, M, COLS), F32),
            pltpu.VMEM((FIELDS, 8, 128), F32),
            pltpu.VMEM((2, FIELDS, 8, 128), F32),
            pltpu.VMEM((8, 128), F32),
            pltpu.VMEM((3, TY // 2, 2, CAP, 128), F32),
            pltpu.VMEM((2, CHUNKS, 128), jnp.int32),
            pltpu.VMEM((2, CHUNKS, 128), F32),
            pltpu.VMEM((CHUNKS, 128, 128), F32),
            pltpu.VMEM((8, NOBS), F32),
            pltpu.VMEM((SLOTS, NOBS), BF16),
            pltpu.VMEM((2 * ROWS, 12, 8, 128), F32),
            dma((FIELDS, ROWS)),
            dma((FIELDS, 2)),
            dma((FIELDS, 2)),
            dma((2, 2)),
            dma((2, 2)),
            dma((len(PARTNERS),)),
            dma((len(PARTNERS),)),
            dma,
            dma,
        ],
        compiler_params=pltpu.CompilerParams(
            collective_id=0, has_side_effects=True, vmem_limit_bytes=40 << 20
        ),
    )(
        ensemble.reshape(M, FIELDS * ROWS, 1, COLS),
        courant_x.reshape(2 * ROWS, COLS),
        courant_y.reshape(2 * ROWS, COLS),
        diffusion,
        mixing,
        growth.reshape(2 * ROWS, COLS),
        land_sea,
        obs_cell,
        obs_value,
        observation_variance,
        obs_perturb,
        radius,
    )
    most = SLOTS // BLOCK
    out = pl.pallas_call(
        analysis_kernel,
        out_shape=shape((M, FIELDS * ROWS, 1, COLS), F32),
        in_specs=[vmem] * 6 + [smem],
        out_specs=hbm,
        scratch_shapes=[
            pltpu.VMEM((FIELDS * ROWS, M, COLS), F32),
            pltpu.VMEM((3, SLOTS, 128), BF16),
            pltpu.VMEM((2, most, BLOCK, 128), BF16),
            pltpu.VMEM((most, BLOCK, 128), F32),
            pltpu.VMEM((most, BLOCK, 128), F32),
            pltpu.VMEM((2, most, 2 * M, 2 * BLOCK), BF16),
            pltpu.VMEM((8, 128), F32),
            pltpu.VMEM((2, most, BLOCK, ROWS * COLS), F32),
            pltpu.VMEM((FIELDS, 128, ROWS * COLS), BF16),
            dma((FIELDS * ROWS,)),
        ],
        compiler_params=pltpu.CompilerParams(vmem_limit_bytes=40 << 20),
    )(x, slots, tab, rows, count, land_sea, radius)
    return out.reshape(ensemble.shape)


def solution(mesh):
    placed = (
        P(None, None, "gy", "gx"),
        P(None, "gy", "gx"),
        P(None, "gy", "gx"),
        P("gy", "gx"),
        P("gy", "gx"),
        P(None, "gy", "gx"),
        P("gy", "gx"),
        P(),
        P(),
        P(),
        P(),
        P(),
    )
    return jax.shard_map(
        local, mesh=mesh, in_specs=placed, out_specs=P(None, None, "gy", "gx"), check_vma=False
    )
```

```python
import functools

import jax
import jax.numpy as jnp
from jax import lax
from jax.experimental import pallas as pl
from jax.experimental.pallas import tpu as pltpu
from jax.sharding import PartitionSpec as P

MESH = pl.DeviceIdType.MESH
F32 = jnp.float32
BF16 = jnp.bfloat16
M = 40
FIELDS = 8
ROWS = 4
COLS = 128
TX = 32
TY = 16
NX = 4096
NOBS = 1024
CAP = 8
SLOTS = 3 * TY * CAP
CHUNKS = NOBS // 128
BLOCK = 128
ORDER = (1, 0, 2, 3, 4, 5, 6, 7)
EARLY = 5
PARTNERS = [
    (dc, dj) for dj in (4, 3, 5, 2, 6, 1, 7, 0) for dc in (1, -1, 0) if (dc, dj) != (0, 0)
]


def dot(a, b):
    return lax.dot_general(a, b, (((1,), (0,)), ((), ())), preferred_element_type=F32)


def dot_t(a, b):
    return lax.dot_general(a, b, (((1,), (1,)), ((), ())), preferred_element_type=F32)


def split3(x):
    high = x.astype(BF16)
    rest = x - high.astype(F32)
    mid = rest.astype(BF16)
    low = (rest - mid.astype(F32)).astype(BF16)
    return high, mid, low


def iota(shape, dim):
    return lax.broadcasted_iota(jnp.int32, shape, dim)


def forecast_kernel(
    ens_ref,
    cx_hbm,
    cy_hbm,
    diff_hbm,
    mix_hbm,
    growth_hbm,
    land_hbm,
    cell_hbm,
    value_hbm,
    var_hbm,
    pert_hbm,
    radius_ref,
    x_ref,
    slots_ref,
    tab_ref,
    row_ref,
    count_ref,
    y_ref,
    halo_ref,
    edge_ref,
    side_ref,
    rec_ref,
    got_ref,
    cell_s,
    rank_s,
    trans_s,
    v_ref,
    hot_ref,
    coef_ref,
    cx_ref,
    cy_ref,
    diff_ref,
    mix_ref,
    growth_ref,
    land_ref,
    cell_ref,
    value_ref,
    var_ref,
    pert_ref,
    small_sem,
    load_sem,
    halo_send,
    halo_recv,
    edge_send,
    edge_recv,
    rec_send,
    rec_recv,
    swap_send,
    swap_recv,
):
    gx = lax.axis_index("gx")
    gy = lax.axis_index("gy")
    core = lax.rem(gy, 2)
    above = (gx, lax.rem(gy + TY - 1, TY))
    below = (gx, lax.rem(gy + 1, TY))
    left = (lax.rem(gx + TX - 1, TX), gy)
    right = (lax.rem(gx + 1, TX), gy)
    sibling = (gx, gy + 1 - 2 * core)

    def partner(dc, dj):
        return (lax.rem(gx + dc + TX, TX), lax.rem(gy + 2 * dj, TY))

    barrier = pltpu.get_barrier_semaphore()
    for device in [partner(dc, dj) for dc, dj in PARTNERS] + [above, below]:
        pl.semaphore_signal(barrier, inc=1, device_id=device, device_id_type=MESH)

    loads = []
    for f in ORDER:
        for r in range(ROWS):
            copy = pltpu.make_async_copy(
                ens_ref.at[:, f * ROWS + r, 0, :], y_ref.at[f, r], load_sem.at[f, r]
            )
            copy.start()
            loads.append(copy)

    sub = iota((8, 128), 0)
    lane = iota((8, 128), 1)
    smalls = []
    for i, (source, target) in enumerate(
        (
            (land_hbm, land_ref),
            (cx_hbm, cx_ref),
            (cy_hbm, cy_ref),
            (diff_hbm, diff_ref),
            (mix_hbm, mix_ref),
            (growth_hbm, growth_ref),
            (cell_hbm, cell_ref),
            (value_hbm, value_ref),
            (var_hbm, var_ref),
            (pert_hbm, pert_ref),
        )
    ):
        copy = pltpu.make_async_copy(source, target, small_sem.at[i])
        copy.start()
        smalls.append(copy)

    for n, f in enumerate(ORDER):
        for r in range(ROWS):
            loads[n * ROWS + r].wait()
        packed = jnp.zeros((8, 128), F32)
        for r in range(ROWS):
            for i in range(M // 8):
                at = 4 * (r * (M // 8) + i)
                moved = pltpu.roll(y_ref[f, r, 8 * i : 8 * i + 8, :], (at + 2) % 128, 1)
                packed = jnp.where((lane >= at) & (lane < at + 4), moved, packed)
        edge_ref[n] = packed

    pl.semaphore_wait(barrier, len(PARTNERS) + 2)

    halos = {}

    def send_rows(f):
        for side, (device, start) in enumerate(((below, 2), (above, 0))):
            copy = pltpu.make_async_remote_copy(
                src_ref=y_ref.at[f, pl.ds(start, 2)],
                dst_ref=halo_ref.at[f, side],
                send_sem=halo_send.at[f, side],
                recv_sem=halo_recv.at[f, side],
                device_id=device,
                device_id_type=MESH,
            )
            copy.start()
            halos[f, side] = copy

    edges = {}

    def send_edges(part, window):
        for side, device in enumerate((right, left)):
            copy = pltpu.make_async_remote_copy(
                src_ref=edge_ref.at[window],
                dst_ref=side_ref.at[side, window],
                send_sem=edge_send.at[part, side],
                recv_sem=edge_recv.at[part, side],
                device_id=device,
                device_id_type=MESH,
            )
            copy.start()
            edges[part, side] = copy

    send_rows(ORDER[0])
    send_edges(0, pl.ds(0, 1))
    send_edges(1, pl.ds(1, FIELDS - 1))
    for f in ORDER[1:EARLY]:
        send_rows(f)

    for copy in smalls:
        copy.wait()

    ocean = land_ref[...].astype(F32)
    first = gy == 0
    last = gy == TY - 1
    for level in range(2):
        for r in range(ROWS):
            at = level * ROWS + r
            o = ocean[r : r + 1, :]
            d = diff_ref[r : r + 1, :] * o
            cx = cx_ref[at : at + 1, :] * o
            cy = cy_ref[at : at + 1, :] * o
            xp, xn = jnp.maximum(cx, 0.0), jnp.minimum(cx, 0.0)
            yp, yn = jnp.maximum(cy, 0.0), jnp.minimum(cy, 0.0)
            terms = [
                1.0 + 0.5 * (xn - xp + yn - yp) - 4.0 * d,
                xn / 6.0,
                d - xp / 3.0 - xn,
                d + xp + xn / 3.0,
                -xp / 6.0,
                yn / 6.0,
                d - yp / 3.0 - yn,
                d + yp + yn / 3.0,
                -yp / 6.0,
            ]
            if r == 0:
                terms[7] = jnp.where(first, 0.0, terms[7])
            if r <= 1:
                terms[8] = jnp.where(first, 0.0, terms[8])
            if r == 3:
                terms[6] = jnp.where(last, 0.0, terms[6])
            if r >= 2:
                terms[5] = jnp.where(last, 0.0, terms[5])
            for i, term in enumerate(terms):
                coef_ref[at, i] = jnp.broadcast_to(term, (8, 128))
            coef_ref[at, 9] = jnp.broadcast_to(o * mix_ref[r : r + 1, :], (8, 128))
            coef_ref[at, 10] = jnp.broadcast_to(o, (8, 128))
            coef_ref[at, 11] = jnp.broadcast_to(growth_ref[at : at + 1, :], (8, 128))

    col_start = gx * COLS
    row_start = gy * ROWS
    me = gx * TY + gy
    big_sub = iota((128, 128), 0)
    big_lane = iota((128, 128), 1)
    own_hot = []
    places = []
    for b in range(2):
        for j in range(CHUNKS):
            cell_s[b, j : j + 1, :] = cell_ref[b : b + 1, 128 * j : 128 * j + 128]
        cell = cell_s[b]
        row = cell >> 12
        col = cell & (NX - 1)
        tile_col = col >> 7
        owner = (tile_col * TY + (row >> 2)).astype(F32)
        for i in range(CHUNKS):
            trans_s[i] = jnp.broadcast_to(owner[i : i + 1, :], (128, 128)).T
        for j in range(CHUNKS):
            mine = jnp.broadcast_to(owner[j : j + 1, :], (128, 128))
            total = jnp.where((trans_s[j] == mine) & (big_sub < big_lane), 1.0, 0.0)
            for i in range(j):
                total = total + jnp.where(trans_s[i] == mine, 1.0, 0.0)
            rank_s[b, j : j + 1, :] = jnp.sum(total, axis=0, keepdims=True)
        rank = rank_s[b]
        own_slot = jnp.where(owner == me.astype(F32), rank, -1.0)
        local_cell = ((row - row_start) * COLS + (col - col_start)).astype(F32)
        subf = sub.astype(F32)
        spot = jnp.zeros((8, 128), F32)
        fill = jnp.zeros((8, 128), F32)
        for j in range(CHUNKS):
            hit = subf == own_slot[j : j + 1, :]
            spot = spot + jnp.where(hit, local_cell[j : j + 1, :], 0.0)
            fill = fill + jnp.where(hit, 1.0, 0.0)
        spot = jnp.sum(spot, axis=1, keepdims=True)
        fill = jnp.sum(fill, axis=1, keepdims=True)
        lane512 = iota((8, ROWS * COLS), 1).astype(F32)
        own_hot.append(jnp.where((spot == lane512) & (fill > 0.0), 1.0, 0.0))
        places.append((row, col, tile_col, rank))
    own_hot = jnp.concatenate(own_hot, axis=0).astype(BF16)

    reach = radius_ref[0] * radius_ref[0]
    upper = jnp.where(big_sub < big_lane, 1.0, 0.0).astype(BF16)

    def before(flag):
        flag = jnp.where(flag, 1.0, 0.0)
        inside = dot(flag.astype(BF16), upper)
        own = jnp.broadcast_to(jnp.sum(flag, axis=1, keepdims=True), (8, 128))
        run = own
        for step in (1, 2, 4):
            run = run + jnp.where(sub >= step, pltpu.roll(run, step, 0), 0.0)
        return inside + run - own, run[7:8, :]

    count_ref[3:4, :] = jnp.full((1, 128), reach, jnp.int32).astype(F32)
    count_ref[4:8, :] = ocean
    for b in range(2):
        row, col, tile_col, rank = places[b]
        relative = (tile_col - gx + 33) & (TX - 1)
        slot = ((relative * TY + (row >> 2)) * CAP).astype(F32) + rank
        offset = ((col - (col_start + 64) + 2048 + NX) & (NX - 1)) - 2048
        gap_x = jnp.maximum(0, jnp.maximum(offset - 63, -64 - offset))
        gap_y = jnp.maximum(0, jnp.maximum(row - (row_start + 3), row_start - row))
        gap = gap_x * gap_x + gap_y * gap_y
        near = gap < reach
        place, count = before(near)
        place = jnp.where(near, place, -1.0)
        count_ref[2 * b : 2 * b + 1, :] = count
        if b == 0:
            beyond = (gap >= reach) & (gap < 4 * reach)
            place2, count2 = before(beyond)
            place = jnp.where(beyond, place2 + count, place)
            count_ref[1:2, :] = count + count2
        v_ref[0:1, :] = value_ref[b : b + 1, :]
        v_ref[1:2, :] = var_ref[b : b + 1, :]
        rowf, colf = row.astype(F32), col.astype(F32)
        for j in range(CHUNKS):
            window = slice(128 * j, 128 * j + 128)
            v_ref[2:3, window] = rowf[j : j + 1, :]
            v_ref[3:4, window] = colf[j : j + 1, :]
            v_ref[4:5, window] = slot[j : j + 1, :]
        v_ref[5:8, :] = jnp.ones((3, NOBS), F32)
        index = iota((SLOTS, 128), 0).astype(F32)
        for j in range(CHUNKS):
            hot = jnp.where(index == place[j : j + 1, :], 1.0, 0.0)
            hot_ref[:, 128 * j : 128 * j + 128] = hot.astype(BF16)
        hot = hot_ref[...]
        vs = split3(v_ref[...])
        column = dot_t(hot, vs[0]) + dot_t(hot, vs[1]) + dot_t(hot, vs[2])
        row_ref[b] = dot_t(vs[0], hot) + dot_t(vs[1], hot) + dot_t(vs[2], hot)
        ps = split3(pert_ref[b])
        noise = dot_t(hot, ps[0]) + dot_t(hot, ps[1]) + dot_t(hot, ps[2])
        tab_ref[b] = jnp.zeros((SLOTS, 128), F32)
        tab_ref[b, :, 0:M] = column[:, 0:1] + jnp.sqrt(column[:, 1:2]) * noise
        tab_ref[b, :, M : M + 8] = column

    def by_member(value, r, at):
        return jnp.broadcast_to(coef_ref[at, value][None], (M // 8, 8, 128)).reshape(M, 128)

    wide_lane = iota((M, 128), 1)

    def inner(n, f):
        level, tracer = divmod(f, 4)
        base = level * 4
        merged = jnp.where((lane & 3) < 2, side_ref[0, n], side_ref[1, n])
        for r in range(ROWS):
            at = level * ROWS + r
            c = functools.partial(by_member, r=r, at=at)
            q = y_ref[f, r]
            halo = jnp.concatenate(
                [
                    pltpu.roll(merged, (126 - 4 * (r * (M // 8) + i)) % 128, 1)
                    for i in range(M // 8)
                ],
                axis=0,
            )
            total = q * c(0)
            total += c(1) * pltpu.roll(jnp.where(wide_lane < 2, halo, q), 126, 1)
            total += c(2) * pltpu.roll(jnp.where(wide_lane < 1, halo, q), 127, 1)
            total += c(3) * pltpu.roll(jnp.where(wide_lane > 126, halo, q), 1, 1)
            total += c(4) * pltpu.roll(jnp.where(wide_lane > 125, halo, q), 2, 1)
            for value, shift in ((5, 2), (6, 1), (7, -1), (8, -2)):
                if 0 <= r + shift < ROWS:
                    total += c(value) * y_ref[f, r + shift]
            total += c(9) * (y_ref[(1 - level) * 4 + tracer, r] - q)
            plankton = y_ref[base + 1, r]
            grazer = y_ref[base + 2, r]
            uptake = grazing = 0.0
            if tracer in (0, 1):
                nutrient = jnp.abs(y_ref[base, r])
                uptake = c(11) * nutrient / (nutrient + 0.5) * plankton
            if tracer in (1, 2, 3):
                size = jnp.abs(plankton)
                grazing = 0.3 * grazer * size / (size + 0.5)
            if tracer == 0:
                change = 0.1 * y_ref[base + 3, r] - uptake
            elif tracer == 1:
                change = uptake - grazing - 0.05 * plankton
            elif tracer == 2:
                change = 0.3 * grazing - 0.05 * grazer
            else:
                change = 0.7 * grazing + 0.05 * plankton + 0.05 * grazer - 0.1 * q
            x_ref[f * ROWS + r] = total + c(10) * change

    def outer(f):
        at = f // 4 * ROWS
        far, near = halo_ref[f, 0, 0], halo_ref[f, 0, 1]
        x_ref[f * ROWS] += by_member(8, 0, at) * far + by_member(7, 0, at) * near
        x_ref[f * ROWS + 1] += by_member(8, 1, at + 1) * near
        near, far = halo_ref[f, 1, 0], halo_ref[f, 1, 1]
        x_ref[f * ROWS + 2] += by_member(5, 2, at + 2) * near
        x_ref[f * ROWS + 3] += by_member(5, 3, at + 3) * far + by_member(6, 3, at + 3) * near

    f = ORDER[0]
    for side in range(2):
        edges[0, side].wait_recv()
    inner(0, f)
    for side in range(2):
        halos[f, side].wait_recv()
    outer(f)

    fields = jnp.concatenate(
        [
            jnp.concatenate(
                [x_ref[f * ROWS + r], jnp.broadcast_to(ocean[r : r + 1, :], (8, 128))], axis=0
            )
            for r in range(ROWS)
        ],
        axis=1,
    )
    high, mid, low = split3(fields)
    prior = dot_t(own_hot, high) + dot_t(own_hot, mid) + dot_t(own_hot, low)
    rec_ref[...] = jnp.zeros((8, 128), F32)
    rec_ref[:, 0:48] = prior[0:8]
    rec_ref[:, 64:112] = prior[8:16]
    half = gy // 2
    got_ref[1, half, core] = rec_ref[...]
    records = []
    for i, (dc, dj) in enumerate(PARTNERS):
        copy = pltpu.make_async_remote_copy(
            src_ref=rec_ref,
            dst_ref=got_ref.at[1 - dc, half, core],
            send_sem=rec_send.at[i],
            recv_sem=rec_recv.at[i],
            device_id=partner(dc, dj),
            device_id_type=MESH,
        )
        copy.start()
        records.append(copy)
    for f in ORDER[EARLY:]:
        send_rows(f)

    for side in range(2):
        edges[1, side].wait_recv()
    for n, f in enumerate(ORDER):
        if n:
            inner(n, f)
    for f in ORDER[1:EARLY]:
        for side in range(2):
            halos[f, side].wait_recv()
        outer(f)
    for copy in records:
        copy.wait_recv()
    swap = pltpu.make_async_remote_copy(
        src_ref=got_ref.at[:, :, core],
        dst_ref=got_ref.at[:, :, core],
        send_sem=swap_send,
        recv_sem=swap_recv,
        device_id=sibling,
        device_id_type=MESH,
    )
    swap.start()
    for f in ORDER[EARLY:]:
        for side in range(2):
            halos[f, side].wait_recv()
        outer(f)
    swap.wait_recv()
    slots_ref[...] = got_ref[...].reshape(SLOTS, 128)
    swap.wait_send()
    for copy in records:
        copy.wait_send()
    for f in ORDER:
        for side in range(2):
            halos[f, side].wait_send()
    for part in range(2):
        for side in range(2):
            edges[part, side].wait_send()


def analysis_kernel(
    x_ref,
    slots_ref,
    tab_ref,
    row_ref,
    count_ref,
    out_ref,
    state_ref,
    part_ref,
    anom_ref,
    scaled_ref,
    innov_ref,
    lhs_ref,
    weight_ref,
    dev_ref,
    out_sem,
):
    gx = lax.axis_index("gx")
    gy = lax.axis_index("gy")
    per_square = 1.0 / count_ref[3:4, :]
    lane = iota((BLOCK, 128), 1)
    member = lane < M
    counts = [jnp.max(count_ref[i : i + 1, :]).astype(jnp.int32) for i in range(3)]
    blocks0, blocks0_wide, blocks1 = [(n + BLOCK - 1) // BLOCK for n in counts]
    for i, piece in enumerate(split3(slots_ref[...])):
        part_ref[i] = piece
    ocean = count_ref[4:8, :]
    exact = functools.partial(
        lax.dot_general, precision=lax.Precision.HIGHEST, preferred_element_type=F32
    )

    def near_x(gap):
        gap = jnp.where(gap >= NX / 2, gap - NX, gap)
        return jnp.where(gap < -NX / 2, gap + NX, gap)

    def load(b, j):
        start = pl.multiple_of(j * BLOCK, BLOCK)
        tab = tab_ref[b, pl.ds(start, BLOCK), :]
        slot = tab[:, M + 4 : M + 5]
        hot = jnp.where(iota((BLOCK, SLOTS), 1).astype(F32) == slot, 1.0, 0.0).astype(BF16)
        prior = dot(hot, part_ref[0]) + dot(hot, part_ref[1]) + dot(hot, part_ref[2])
        if b:
            prior = pltpu.roll(prior, 64, 1)
        return tab, prior

    def finish(b, j, tab, prior):
        prior = jnp.where(member, prior, 0.0)
        anomaly = jnp.where(
            member, prior - jnp.sum(prior, axis=1, keepdims=True) * (1.0 / M), 0.0
        )
        spread = jnp.sum(anomaly * anomaly, axis=1, keepdims=True) * (1.0 / (M - 1))
        filled = tab[:, M + 5 : M + 6]
        scale = filled / ((M - 1) * (spread + tab[:, M + 1 : M + 2] + (1.0 - filled)))
        innovation = jnp.where(member, tab, 0.0) - prior
        if b == 0:
            scaled_ref[j] = anomaly * scale
            innov_ref[j] = innovation
        high = anomaly.astype(BF16).astype(F32)
        lhs = high + pltpu.roll(high, M, 1) + pltpu.roll(anomaly - high, 2 * M, 1)
        anom_ref[b, j] = lhs.astype(BF16)
        turned = innovation.T[0:M, :]
        high = turned.astype(BF16).astype(F32)
        lhs = jnp.concatenate(
            [
                jnp.concatenate([high, high], axis=1),
                jnp.concatenate([turned - high, jnp.zeros_like(high)], axis=1),
            ],
            axis=0,
        )
        lhs_ref[b, j] = lhs.astype(BF16)
        gap = near_x(tab[:, M + 3 : M + 4] - (gx * COLS + lane).astype(F32))
        square = gap * gap
        for r in range(ROWS):
            gap = tab[:, M + 2 : M + 3] - (gy * ROWS + r).astype(F32)
            taper = jnp.maximum(0.0, 1.0 - (square + gap * gap) * per_square)
            weight_ref[b, j, :, 128 * r : 128 * r + 128] = taper * scale

    def first_batch(j, carry):
        tab, prior = load(0, j)
        finish(0, j, tab, prior)
        return carry

    first_batch(0, 0)
    lax.fori_loop(1, blocks0_wide, first_batch, 0)

    def deviation_of(prior):
        inside = jnp.where(member, prior, 0.0)
        mean = jnp.sum(inside, axis=1, keepdims=True) * (1.0 / M)
        return inside, jnp.where(member, inside - mean, 0.0)

    def effect(i, tab, deviation):
        cover = exact(deviation, scaled_ref[i], (((1,), (1,)), ((), ())))
        window = pl.ds(pl.multiple_of(i * BLOCK, BLOCK), BLOCK)
        gap_x = near_x(row_ref[0, 3:4, window] - tab[:, M + 3 : M + 4])
        gap_y = row_ref[0, 2:3, window] - tab[:, M + 2 : M + 3]
        taper = jnp.maximum(0.0, 1.0 - (gap_x * gap_x + gap_y * gap_y) * per_square)
        return exact(cover * taper, innov_ref[i], (((1,), (0,)), ((), ())))

    def second_batch(j, carry):
        tab, prior = load(1, j)
        inside, deviation = deviation_of(prior)
        total = lax.fori_loop(
            1,
            blocks0_wide,
            lambda i, total: total + effect(i, tab, deviation),
            effect(0, tab, deviation),
        )
        finish(1, j, tab, inside + prior[:, M : M + 1] * total)
        return carry

    def spread_field(b, source, f):
        for r in range(ROWS):
            x = source[f * ROWS + r]
            deviation = x - jnp.sum(x, axis=0, keepdims=True) * (1.0 / M)
            high = deviation.astype(BF16).astype(F32)
            stack = jnp.concatenate(
                [high, deviation - high, high, jnp.zeros((8, 128), F32)], axis=0
            )
            dev_ref[b, f, :, 128 * r : 128 * r + 128] = stack.astype(BF16)

    def increment(b, j, f):
        cover = dot(anom_ref[b, j], dev_ref[b, f])
        gain = cover * weight_ref[b, j]
        high = gain.astype(BF16)
        low = (gain - high.astype(F32)).astype(BF16)
        both = dot(lhs_ref[b, j], jnp.concatenate([high, low], axis=0))
        return both[0:M] + both[M : 2 * M]

    def apply_field(b, source, f):
        spread_field(b, source, f)
        change = increment(b, 0, f)
        for r in range(ROWS):
            state_ref[f * ROWS + r] = (
                source[f * ROWS + r] + ocean[r : r + 1, :] * change[:, 128 * r : 128 * r + 128]
            )

    def store(f):
        for r in range(ROWS):
            i = f * ROWS + r
            pltpu.make_async_copy(state_ref.at[i], out_ref.at[:, i, 0, :], out_sem.at[i]).start()

    short = (blocks0 <= 1) & (blocks1 <= 1)

    @pl.when(short)
    def _():
        tab, prior = load(1, 0)
        inside, deviation = deviation_of(prior)
        extra = lax.fori_loop(
            1,
            blocks0_wide,
            lambda i, total: total + effect(i, tab, deviation),
            jnp.zeros((BLOCK, 128), F32),
        )
        total = extra + effect(0, tab, deviation)
        finish(1, 0, tab, inside + prior[:, M : M + 1] * total)
        for f in range(FIELDS):
            apply_field(0, x_ref, f)
        for f in range(FIELDS):
            apply_field(1, state_ref, f)
            store(f)

    @pl.when(jnp.logical_not(short))
    def _():
        second_batch(0, 0)
        lax.fori_loop(1, blocks1, second_batch, 0)
        for b, blocks, source in ((0, blocks0, x_ref), (1, blocks1, state_ref)):

            def field(f, carry, b=b, source=source):
                apply_field(b, source, f)
                return carry

            lax.fori_loop(0, FIELDS, field, 0)

            def more(j, carry, b=b):
                def field_more(f, inner_carry):
                    change = increment(b, j, f)
                    for r in range(ROWS):
                        state_ref[f * ROWS + r] += (
                            ocean[r : r + 1, :] * change[:, 128 * r : 128 * r + 128]
                        )
                    return inner_carry

                return lax.fori_loop(0, FIELDS, field_more, carry)

            lax.fori_loop(1, blocks, more, 0)
        for f in range(FIELDS):
            store(f)

    for i in range(FIELDS * ROWS):
        pltpu.make_async_copy(state_ref.at[i], out_ref.at[:, i, 0, :], out_sem.at[i]).wait()


def local(
    ensemble,
    courant_x,
    courant_y,
    diffusion,
    mixing,
    growth,
    land_sea,
    obs_cell,
    obs_value,
    observation_variance,
    obs_perturb,
    radius,
):
    vmem = pl.BlockSpec(memory_space=pltpu.VMEM)
    hbm = pl.BlockSpec(memory_space=pltpu.HBM)
    shape = jax.ShapeDtypeStruct
    dma = pltpu.SemaphoreType.DMA
    x, slots, tab, rows, count = pl.pallas_call(
        forecast_kernel,
        out_shape=(
            shape((FIELDS * ROWS, M, COLS), F32),
            shape((SLOTS, 128), F32),
            shape((2, SLOTS, 128), F32),
            shape((2, 8, SLOTS), F32),
            shape((8, 128), F32),
        ),
        in_specs=[hbm] * 11 + [pl.BlockSpec(memory_space=pltpu.SMEM)],
        out_specs=(vmem,) * 5,
        scratch_shapes=[
            pltpu.VMEM((FIELDS, ROWS, M, COLS), F32),
            pltpu.VMEM((FIELDS, 2, 2, M, COLS), F32),
            pltpu.VMEM((FIELDS, 8, 128), F32),
            pltpu.VMEM((2, FIELDS, 8, 128), F32),
            pltpu.VMEM((8, 128), F32),
            pltpu.VMEM((3, TY // 2, 2, CAP, 128), F32),
            pltpu.VMEM((2, CHUNKS, 128), jnp.int32),
            pltpu.VMEM((2, CHUNKS, 128), F32),
            pltpu.VMEM((CHUNKS, 128, 128), F32),
            pltpu.VMEM((8, NOBS), F32),
            pltpu.VMEM((SLOTS, NOBS), BF16),
            pltpu.VMEM((2 * ROWS, 12, 8, 128), F32),
            pltpu.VMEM((2 * ROWS, COLS), F32),
            pltpu.VMEM((2 * ROWS, COLS), F32),
            pltpu.VMEM((ROWS, COLS), F32),
            pltpu.VMEM((ROWS, COLS), F32),
            pltpu.VMEM((2 * ROWS, COLS), F32),
            pltpu.VMEM((ROWS, COLS), jnp.int32),
            pltpu.VMEM((2, NOBS), jnp.int32),
            pltpu.VMEM((2, NOBS), F32),
            pltpu.VMEM((2, NOBS), F32),
            pltpu.VMEM((2, M, NOBS), F32),
            dma((10,)),
            dma((FIELDS, ROWS)),
            dma((FIELDS, 2)),
            dma((FIELDS, 2)),
            dma((2, 2)),
            dma((2, 2)),
            dma((len(PARTNERS),)),
            dma((len(PARTNERS),)),
            dma,
            dma,
        ],
        compiler_params=pltpu.CompilerParams(
            collective_id=0, has_side_effects=True, vmem_limit_bytes=40 << 20
        ),
    )(
        *(
            pltpu.with_memory_space_constraint(array, pltpu.HBM)
            for array in (
                ensemble.reshape(M, FIELDS * ROWS, 1, COLS),
                courant_x.reshape(2 * ROWS, COLS),
                courant_y.reshape(2 * ROWS, COLS),
                diffusion,
                mixing,
                growth.reshape(2 * ROWS, COLS),
                land_sea,
                obs_cell,
                obs_value,
                observation_variance,
                jnp.swapaxes(obs_perturb, 1, 2),
            )
        ),
        radius,
    )
    most = SLOTS // BLOCK
    out = pl.pallas_call(
        analysis_kernel,
        out_shape=shape((M, FIELDS * ROWS, 1, COLS), F32),
        in_specs=[vmem] * 5,
        out_specs=hbm,
        scratch_shapes=[
            pltpu.VMEM((FIELDS * ROWS, M, COLS), F32),
            pltpu.VMEM((3, SLOTS, 128), BF16),
            pltpu.VMEM((2, most, BLOCK, 128), BF16),
            pltpu.VMEM((most, BLOCK, 128), F32),
            pltpu.VMEM((most, BLOCK, 128), F32),
            pltpu.VMEM((2, most, 2 * M, 2 * BLOCK), BF16),
            pltpu.VMEM((2, most, BLOCK, ROWS * COLS), F32),
            pltpu.VMEM((2, FIELDS, 128, ROWS * COLS), BF16),
            dma((FIELDS * ROWS,)),
        ],
        compiler_params=pltpu.CompilerParams(vmem_limit_bytes=40 << 20),
    )(x, slots, tab, rows, count)
    return out.reshape(ensemble.shape)


def solution(mesh):
    placed = (
        P(None, None, "gy", "gx"),
        P(None, "gy", "gx"),
        P(None, "gy", "gx"),
        P("gy", "gx"),
        P("gy", "gx"),
        P(None, "gy", "gx"),
        P("gy", "gx"),
        P(),
        P(),
        P(),
        P(),
        P(),
    )
    return jax.shard_map(
        local, mesh=mesh, in_specs=placed, out_specs=P(None, None, "gy", "gx"), check_vma=False
    )
```

```python
import functools

import jax
import jax.numpy as jnp
from jax import lax
from jax.experimental import pallas as pl
from jax.experimental.pallas import tpu as pltpu
from jax.sharding import PartitionSpec as P

MESH = pl.DeviceIdType.MESH
F32 = jnp.float32
BF16 = jnp.bfloat16
M = 40
FIELDS = 8
ROWS = 4
COLS = 128
TX = 32
TY = 16
NX = 4096
NOBS = 1024
CAP = 8
SLOTS = 3 * TY * CAP
CHUNKS = NOBS // 128
BLOCK = 128
WIDE = 2
ORDER = (1, 0, 2, 3, 4, 5, 6, 7)
EARLY = 4
PARTNERS = [
    (dc, dj) for dj in (4, 3, 5, 2, 6, 1, 7, 0) for dc in (1, -1, 0) if (dc, dj) != (0, 0)
]


def dot(a, b):
    return lax.dot_general(a, b, (((1,), (0,)), ((), ())), preferred_element_type=F32)


def dot_t(a, b):
    return lax.dot_general(a, b, (((1,), (1,)), ((), ())), preferred_element_type=F32)


def split3(x):
    high = x.astype(BF16)
    rest = x - high.astype(F32)
    mid = rest.astype(BF16)
    low = (rest - mid.astype(F32)).astype(BF16)
    return high, mid, low


def iota(shape, dim):
    return lax.broadcasted_iota(jnp.int32, shape, dim)


class Analysis:
    def __init__(self, tab, row, count, part, anom, scaled, innov, lhs, weight, dev, state):
        self.tab, self.row, self.part = tab, row, part
        self.anom, self.scaled, self.innov = anom, scaled, innov
        self.lhs, self.weight, self.dev, self.state = lhs, weight, dev, state
        self.gx, self.gy = lax.axis_index("gx"), lax.axis_index("gy")
        self.lane = iota((BLOCK, 128), 1)
        self.member = self.lane < M
        self.per_square = 1.0 / count[3:4, :]
        self.ocean = count[4:8, :]
        self.exact = functools.partial(
            lax.dot_general, precision=lax.Precision.HIGHEST, preferred_element_type=F32
        )

    def near_x(self, gap):
        gap = jnp.where(gap >= NX / 2, gap - NX, gap)
        return jnp.where(gap < -NX / 2, gap + NX, gap)

    def load(self, b, j):
        start = j * BLOCK if isinstance(j, int) else pl.multiple_of(j * BLOCK, BLOCK)
        tab = self.tab[b, pl.ds(start, BLOCK), :]
        slot = tab[:, M + 4 : M + 5]
        hot = jnp.where(iota((BLOCK, SLOTS), 1).astype(F32) == slot, 1.0, 0.0).astype(BF16)
        prior = dot(hot, self.part[0]) + dot(hot, self.part[1]) + dot(hot, self.part[2])
        if b:
            prior = pltpu.roll(prior, 64, 1)
        return tab, prior

    def deviation_of(self, prior):
        inside = jnp.where(self.member, prior, 0.0)
        mean = jnp.sum(inside, axis=1, keepdims=True) * (1.0 / M)
        return inside, jnp.where(self.member, inside - mean, 0.0)

    def finish(self, b, j, tab, prior, grid=True):
        prior, anomaly = self.deviation_of(prior)
        spread = jnp.sum(anomaly * anomaly, axis=1, keepdims=True) * (1.0 / (M - 1))
        filled = tab[:, M + 5 : M + 6]
        scale = filled / ((M - 1) * (spread + tab[:, M + 1 : M + 2] + (1.0 - filled)))
        innovation = jnp.where(self.member, tab, 0.0) - prior
        if b == 0:
            self.scaled[j] = anomaly * scale
            self.innov[j] = innovation
        if not grid:
            return
        high = anomaly.astype(BF16).astype(F32)
        lhs = high + pltpu.roll(high, M, 1) + pltpu.roll(anomaly - high, 2 * M, 1)
        self.anom[b, j] = lhs.astype(BF16)
        turned = innovation.T[0:M, :]
        high = turned.astype(BF16).astype(F32)
        lhs = jnp.concatenate(
            [
                jnp.concatenate([high, high], axis=1),
                jnp.concatenate([turned - high, jnp.zeros_like(high)], axis=1),
            ],
            axis=0,
        )
        self.lhs[b, j] = lhs.astype(BF16)
        gap = self.near_x(tab[:, M + 3 : M + 4] - (self.gx * COLS + self.lane).astype(F32))
        square = gap * gap
        for r in range(ROWS):
            gap = tab[:, M + 2 : M + 3] - (self.gy * ROWS + r).astype(F32)
            taper = jnp.maximum(0.0, 1.0 - (square + gap * gap) * self.per_square)
            self.weight[b, j, :, 128 * r : 128 * r + 128] = taper * scale

    def effect(self, i, tab, deviation):
        cover = self.exact(deviation, self.scaled[i], (((1,), (1,)), ((), ())))
        start = i * BLOCK if isinstance(i, int) else pl.multiple_of(i * BLOCK, BLOCK)
        window = pl.ds(start, BLOCK)
        gap_x = self.near_x(self.row[0, 3:4, window] - tab[:, M + 3 : M + 4])
        gap_y = self.row[0, 2:3, window] - tab[:, M + 2 : M + 3]
        taper = jnp.maximum(0.0, 1.0 - (gap_x * gap_x + gap_y * gap_y) * self.per_square)
        return self.exact(cover * taper, self.innov[i], (((1,), (0,)), ((), ())))

    def spread_field(self, b, source, f):
        for r in range(ROWS):
            x = source[f * ROWS + r]
            deviation = x - jnp.sum(x, axis=0, keepdims=True) * (1.0 / M)
            high = deviation.astype(BF16).astype(F32)
            stack = jnp.concatenate(
                [high, deviation - high, high, jnp.zeros((8, 128), F32)], axis=0
            )
            self.dev[b, f, :, 128 * r : 128 * r + 128] = stack.astype(BF16)

    def increment(self, b, j, f):
        cover = dot(self.anom[b, j], self.dev[b, f])
        gain = cover * self.weight[b, j]
        high = gain.astype(BF16)
        low = (gain - high.astype(F32)).astype(BF16)
        both = dot(self.lhs[b, j], jnp.concatenate([high, low], axis=0))
        return both[0:M] + both[M : 2 * M]

    def apply_field(self, b, source, f):
        change = self.increment(b, 0, f)
        for r in range(ROWS):
            self.state[f * ROWS + r] = (
                source[f * ROWS + r]
                + self.ocean[r : r + 1, :] * change[:, 128 * r : 128 * r + 128]
            )


def analysis_kernel(
    done_ref,
    x_ref,
    slots_ref,
    tab_ref,
    row_ref,
    count_ref,
    out_ref,
    part_ref,
    anom_ref,
    scaled_ref,
    innov_ref,
    lhs_ref,
    weight_ref,
    dev_ref,
    state_ref,
    out_sem,
):
    def stores(source):
        for i in range(FIELDS * ROWS):
            yield pltpu.make_async_copy(source.at[i], out_ref.at[:, i, 0, :], out_sem.at[i])

    for copy in stores(done_ref):
        copy.start()
    counts = [jnp.max(count_ref[i : i + 1, :]).astype(jnp.int32) for i in range(3)]
    blocks0, blocks0_wide, blocks1 = [(n + BLOCK - 1) // BLOCK for n in counts]
    for copy in stores(done_ref):
        copy.wait()

    @pl.when((blocks0 > 1) | (blocks0_wide > WIDE) | (blocks1 > 1))
    def _():
        a = Analysis(
            tab_ref, row_ref, count_ref, part_ref, anom_ref, scaled_ref, innov_ref, lhs_ref,
            weight_ref, dev_ref, state_ref,
        )
        for i, piece in enumerate(split3(slots_ref[...])):
            part_ref[i] = piece

        def first_batch(j, carry):
            a.finish(0, j, *a.load(0, j))
            return carry

        lax.fori_loop(0, blocks0_wide, first_batch, 0)

        def second_batch(j, carry):
            tab, prior = a.load(1, j)
            inside, deviation = a.deviation_of(prior)
            total = lax.fori_loop(
                0,
                blocks0_wide,
                lambda i, total: total + a.effect(i, tab, deviation),
                jnp.zeros((BLOCK, 128), F32),
            )
            a.finish(1, j, tab, inside + prior[:, M : M + 1] * total)
            return carry

        lax.fori_loop(0, blocks1, second_batch, 0)
        state_ref[...] = x_ref[...]
        for b, blocks in ((0, blocks0), (1, blocks1)):

            def spread(f, carry, b=b):
                a.spread_field(b, state_ref, f)
                return carry

            lax.fori_loop(0, FIELDS, spread, 0)

            def block(j, carry, b=b):
                def field(f, inner_carry):
                    change = a.increment(b, j, f)
                    for r in range(ROWS):
                        state_ref[f * ROWS + r] += (
                            a.ocean[r : r + 1, :] * change[:, 128 * r : 128 * r + 128]
                        )
                    return inner_carry

                return lax.fori_loop(0, FIELDS, field, carry)

            lax.fori_loop(0, blocks, block, 0)
        for copy in stores(state_ref):
            copy.start()
        for copy in stores(state_ref):
            copy.wait()


def forecast_kernel(
    ens_ref,
    cx_hbm,
    cy_hbm,
    diff_hbm,
    mix_hbm,
    growth_hbm,
    land_hbm,
    cell_hbm,
    value_hbm,
    var_hbm,
    pert_hbm,
    radius_ref,
    done_ref,
    x_ref,
    slots_ref,
    tab_ref,
    row_ref,
    count_ref,
    y_ref,
    halo_ref,
    edge_ref,
    side_ref,
    rec_ref,
    got_ref,
    cell_s,
    rank_s,
    trans_s,
    v_ref,
    hot_ref,
    coef_ref,
    cx_ref,
    cy_ref,
    diff_ref,
    mix_ref,
    growth_ref,
    land_ref,
    cell_ref,
    value_ref,
    var_ref,
    pert_ref,
    part_ref,
    anom_ref,
    scaled_ref,
    innov_ref,
    lhs_ref,
    weight_ref,
    dev_ref,
    small_sem,
    load_sem,
    halo_send,
    halo_recv,
    edge_send,
    edge_recv,
    rec_send,
    rec_recv,
    swap_send,
    swap_recv,
):
    gx = lax.axis_index("gx")
    gy = lax.axis_index("gy")
    core = lax.rem(gy, 2)
    above = (gx, lax.rem(gy + TY - 1, TY))
    below = (gx, lax.rem(gy + 1, TY))
    left = (lax.rem(gx + TX - 1, TX), gy)
    right = (lax.rem(gx + 1, TX), gy)
    sibling = (gx, gy + 1 - 2 * core)

    def partner(dc, dj):
        return (lax.rem(gx + dc + TX, TX), lax.rem(gy + 2 * dj, TY))

    barrier = pltpu.get_barrier_semaphore()
    for device in [partner(dc, dj) for dc, dj in PARTNERS] + [above, below]:
        pl.semaphore_signal(barrier, inc=1, device_id=device, device_id_type=MESH)

    loads = []
    for f in ORDER:
        for r in range(ROWS):
            copy = pltpu.make_async_copy(
                ens_ref.at[:, f * ROWS + r, 0, :], y_ref.at[f, r], load_sem.at[f, r]
            )
            copy.start()
            loads.append(copy)

    sub = iota((8, 128), 0)
    lane = iota((8, 128), 1)
    smalls = []
    for i, (source, target) in enumerate(
        (
            (land_hbm, land_ref),
            (cx_hbm, cx_ref),
            (cy_hbm, cy_ref),
            (diff_hbm, diff_ref),
            (mix_hbm, mix_ref),
            (growth_hbm, growth_ref),
            (cell_hbm, cell_ref),
            (value_hbm, value_ref),
            (var_hbm, var_ref),
            (pert_hbm, pert_ref),
        )
    ):
        copy = pltpu.make_async_copy(source, target, small_sem.at[i])
        copy.start()
        smalls.append(copy)

    for n, f in enumerate(ORDER):
        for r in range(ROWS):
            loads[n * ROWS + r].wait()
        packed = jnp.zeros((8, 128), F32)
        for r in range(ROWS):
            for i in range(M // 8):
                at = 4 * (r * (M // 8) + i)
                moved = pltpu.roll(y_ref[f, r, 8 * i : 8 * i + 8, :], (at + 2) % 128, 1)
                packed = jnp.where((lane >= at) & (lane < at + 4), moved, packed)
        edge_ref[n] = packed

    pl.semaphore_wait(barrier, len(PARTNERS) + 2)

    halos = {}

    def send_rows(f):
        for side, (device, start) in enumerate(((below, 2), (above, 0))):
            copy = pltpu.make_async_remote_copy(
                src_ref=y_ref.at[f, pl.ds(start, 2)],
                dst_ref=halo_ref.at[f, side],
                send_sem=halo_send.at[f, side],
                recv_sem=halo_recv.at[f, side],
                device_id=device,
                device_id_type=MESH,
            )
            copy.start()
            halos[f, side] = copy

    edges = {}

    def send_edges(part, window):
        for side, device in enumerate((right, left)):
            copy = pltpu.make_async_remote_copy(
                src_ref=edge_ref.at[window],
                dst_ref=side_ref.at[side, window],
                send_sem=edge_send.at[part, side],
                recv_sem=edge_recv.at[part, side],
                device_id=device,
                device_id_type=MESH,
            )
            copy.start()
            edges[part, side] = copy

    send_rows(ORDER[0])
    send_edges(0, pl.ds(0, 1))
    send_edges(1, pl.ds(1, FIELDS - 1))
    for f in ORDER[1:EARLY]:
        send_rows(f)

    for copy in smalls:
        copy.wait()

    ocean = land_ref[...].astype(F32)
    first = gy == 0
    last = gy == TY - 1
    for level in range(2):
        for r in range(ROWS):
            at = level * ROWS + r
            o = ocean[r : r + 1, :]
            d = diff_ref[r : r + 1, :] * o
            cx = cx_ref[at : at + 1, :] * o
            cy = cy_ref[at : at + 1, :] * o
            xp, xn = jnp.maximum(cx, 0.0), jnp.minimum(cx, 0.0)
            yp, yn = jnp.maximum(cy, 0.0), jnp.minimum(cy, 0.0)
            terms = [
                1.0 + 0.5 * (xn - xp + yn - yp) - 4.0 * d,
                xn / 6.0,
                d - xp / 3.0 - xn,
                d + xp + xn / 3.0,
                -xp / 6.0,
                yn / 6.0,
                d - yp / 3.0 - yn,
                d + yp + yn / 3.0,
                -yp / 6.0,
            ]
            if r == 0:
                terms[7] = jnp.where(first, 0.0, terms[7])
            if r <= 1:
                terms[8] = jnp.where(first, 0.0, terms[8])
            if r == 3:
                terms[6] = jnp.where(last, 0.0, terms[6])
            if r >= 2:
                terms[5] = jnp.where(last, 0.0, terms[5])
            for i, term in enumerate(terms):
                coef_ref[at, i] = jnp.broadcast_to(term, (8, 128))
            coef_ref[at, 9] = jnp.broadcast_to(o * mix_ref[r : r + 1, :], (8, 128))
            coef_ref[at, 10] = jnp.broadcast_to(o, (8, 128))
            coef_ref[at, 11] = jnp.broadcast_to(growth_ref[at : at + 1, :], (8, 128))

    col_start = gx * COLS
    row_start = gy * ROWS
    me = gx * TY + gy
    big_sub = iota((128, 128), 0)
    big_lane = iota((128, 128), 1)
    own_hot = []
    places = []
    for b in range(2):
        for j in range(CHUNKS):
            cell_s[b, j : j + 1, :] = cell_ref[b : b + 1, 128 * j : 128 * j + 128]
        cell = cell_s[b]
        row = cell >> 12
        col = cell & (NX - 1)
        tile_col = col >> 7
        owner = (tile_col * TY + (row >> 2)).astype(F32)
        for i in range(CHUNKS):
            trans_s[i] = jnp.broadcast_to(owner[i : i + 1, :], (128, 128)).T
        for j in range(CHUNKS):
            mine = jnp.broadcast_to(owner[j : j + 1, :], (128, 128))
            total = jnp.where((trans_s[j] == mine) & (big_sub < big_lane), 1.0, 0.0)
            for i in range(j):
                total = total + jnp.where(trans_s[i] == mine, 1.0, 0.0)
            rank_s[b, j : j + 1, :] = jnp.sum(total, axis=0, keepdims=True)
        rank = rank_s[b]
        own_slot = jnp.where(owner == me.astype(F32), rank, -1.0)
        local_cell = ((row - row_start) * COLS + (col - col_start)).astype(F32)
        subf = sub.astype(F32)
        spot = jnp.zeros((8, 128), F32)
        fill = jnp.zeros((8, 128), F32)
        for j in range(CHUNKS):
            hit = subf == own_slot[j : j + 1, :]
            spot = spot + jnp.where(hit, local_cell[j : j + 1, :], 0.0)
            fill = fill + jnp.where(hit, 1.0, 0.0)
        spot = jnp.sum(spot, axis=1, keepdims=True)
        fill = jnp.sum(fill, axis=1, keepdims=True)
        lane512 = iota((8, ROWS * COLS), 1).astype(F32)
        own_hot.append(jnp.where((spot == lane512) & (fill > 0.0), 1.0, 0.0))
        places.append((row, col, tile_col, rank))
    own_hot = jnp.concatenate(own_hot, axis=0).astype(BF16)

    reach = radius_ref[0] * radius_ref[0]
    upper = jnp.where(big_sub < big_lane, 1.0, 0.0).astype(BF16)

    def before(flag):
        flag = jnp.where(flag, 1.0, 0.0)
        inside = dot(flag.astype(BF16), upper)
        own = jnp.broadcast_to(jnp.sum(flag, axis=1, keepdims=True), (8, 128))
        run = own
        for step in (1, 2, 4):
            run = run + jnp.where(sub >= step, pltpu.roll(run, step, 0), 0.0)
        return inside + run - own, run[7:8, :]

    count_ref[3:4, :] = jnp.full((1, 128), reach, jnp.int32).astype(F32)
    count_ref[4:8, :] = ocean
    for b in range(2):
        row, col, tile_col, rank = places[b]
        relative = (tile_col - gx + 33) & (TX - 1)
        slot = ((relative * TY + (row >> 2)) * CAP).astype(F32) + rank
        offset = ((col - (col_start + 64) + 2048 + NX) & (NX - 1)) - 2048
        gap_x = jnp.maximum(0, jnp.maximum(offset - 63, -64 - offset))
        gap_y = jnp.maximum(0, jnp.maximum(row - (row_start + 3), row_start - row))
        gap = gap_x * gap_x + gap_y * gap_y
        near = gap < reach
        place, count = before(near)
        place = jnp.where(near, place, -1.0)
        count_ref[2 * b : 2 * b + 1, :] = count
        if b == 0:
            beyond = (gap >= reach) & (gap < 4 * reach)
            place2, count2 = before(beyond)
            place = jnp.where(beyond, place2 + count, place)
            count_ref[1:2, :] = count + count2
        v_ref[0:1, :] = value_ref[b : b + 1, :]
        v_ref[1:2, :] = var_ref[b : b + 1, :]
        rowf, colf = row.astype(F32), col.astype(F32)
        for j in range(CHUNKS):
            window = slice(128 * j, 128 * j + 128)
            v_ref[2:3, window] = rowf[j : j + 1, :]
            v_ref[3:4, window] = colf[j : j + 1, :]
            v_ref[4:5, window] = slot[j : j + 1, :]
        v_ref[5:8, :] = jnp.ones((3, NOBS), F32)
        index = iota((SLOTS, 128), 0).astype(F32)
        for j in range(CHUNKS):
            hot = jnp.where(index == place[j : j + 1, :], 1.0, 0.0)
            hot_ref[:, 128 * j : 128 * j + 128] = hot.astype(BF16)
        hot = hot_ref[...]
        vs = split3(v_ref[...])
        column = dot_t(hot, vs[0]) + dot_t(hot, vs[1]) + dot_t(hot, vs[2])
        row_ref[b] = dot_t(vs[0], hot) + dot_t(vs[1], hot) + dot_t(vs[2], hot)
        ps = split3(pert_ref[b])
        noise = dot_t(hot, ps[0]) + dot_t(hot, ps[1]) + dot_t(hot, ps[2])
        tab_ref[b] = jnp.zeros((SLOTS, 128), F32)
        tab_ref[b, :, 0:M] = column[:, 0:1] + jnp.sqrt(column[:, 1:2]) * noise
        tab_ref[b, :, M : M + 8] = column

    def by_member(value, r, at):
        return jnp.broadcast_to(coef_ref[at, value][None], (M // 8, 8, 128)).reshape(M, 128)

    wide_lane = iota((M, 128), 1)

    def inner(n, f):
        level, tracer = divmod(f, 4)
        base = level * 4
        merged = jnp.where((lane & 3) < 2, side_ref[0, n], side_ref[1, n])
        for r in range(ROWS):
            at = level * ROWS + r
            c = functools.partial(by_member, r=r, at=at)
            q = y_ref[f, r]
            halo = jnp.concatenate(
                [
                    pltpu.roll(merged, (126 - 4 * (r * (M // 8) + i)) % 128, 1)
                    for i in range(M // 8)
                ],
                axis=0,
            )
            total = q * c(0)
            total += c(1) * pltpu.roll(jnp.where(wide_lane < 2, halo, q), 126, 1)
            total += c(2) * pltpu.roll(jnp.where(wide_lane < 1, halo, q), 127, 1)
            total += c(3) * pltpu.roll(jnp.where(wide_lane > 126, halo, q), 1, 1)
            total += c(4) * pltpu.roll(jnp.where(wide_lane > 125, halo, q), 2, 1)
            for value, shift in ((5, 2), (6, 1), (7, -1), (8, -2)):
                if 0 <= r + shift < ROWS:
                    total += c(value) * y_ref[f, r + shift]
            total += c(9) * (y_ref[(1 - level) * 4 + tracer, r] - q)
            plankton = y_ref[base + 1, r]
            grazer = y_ref[base + 2, r]
            uptake = grazing = 0.0
            if tracer in (0, 1):
                nutrient = jnp.abs(y_ref[base, r])
                uptake = c(11) * nutrient / (nutrient + 0.5) * plankton
            if tracer in (1, 2, 3):
                size = jnp.abs(plankton)
                grazing = 0.3 * grazer * size / (size + 0.5)
            if tracer == 0:
                change = 0.1 * y_ref[base + 3, r] - uptake
            elif tracer == 1:
                change = uptake - grazing - 0.05 * plankton
            elif tracer == 2:
                change = 0.3 * grazing - 0.05 * grazer
            else:
                change = 0.7 * grazing + 0.05 * plankton + 0.05 * grazer - 0.1 * q
            x_ref[f * ROWS + r] = total + c(10) * change

    def outer(f):
        at = f // 4 * ROWS
        far, near = halo_ref[f, 0, 0], halo_ref[f, 0, 1]
        x_ref[f * ROWS] += by_member(8, 0, at) * far + by_member(7, 0, at) * near
        x_ref[f * ROWS + 1] += by_member(8, 1, at + 1) * near
        near, far = halo_ref[f, 1, 0], halo_ref[f, 1, 1]
        x_ref[f * ROWS + 2] += by_member(5, 2, at + 2) * near
        x_ref[f * ROWS + 3] += by_member(5, 3, at + 3) * far + by_member(6, 3, at + 3) * near

    f = ORDER[0]
    for side in range(2):
        edges[0, side].wait_recv()
    inner(0, f)
    for side in range(2):
        halos[f, side].wait_recv()
    outer(f)

    fields = jnp.concatenate(
        [
            jnp.concatenate(
                [x_ref[f * ROWS + r], jnp.broadcast_to(ocean[r : r + 1, :], (8, 128))], axis=0
            )
            for r in range(ROWS)
        ],
        axis=1,
    )
    high, mid, low = split3(fields)
    prior = dot_t(own_hot, high) + dot_t(own_hot, mid) + dot_t(own_hot, low)
    rec_ref[...] = jnp.zeros((8, 128), F32)
    rec_ref[:, 0:48] = prior[0:8]
    rec_ref[:, 64:112] = prior[8:16]
    half = gy // 2
    got_ref[1, half, core] = rec_ref[...]
    records = []
    for i, (dc, dj) in enumerate(PARTNERS):
        copy = pltpu.make_async_remote_copy(
            src_ref=rec_ref,
            dst_ref=got_ref.at[1 - dc, half, core],
            send_sem=rec_send.at[i],
            recv_sem=rec_recv.at[i],
            device_id=partner(dc, dj),
            device_id_type=MESH,
        )
        copy.start()
        records.append(copy)

    for side in range(2):
        edges[1, side].wait_recv()
    for n, f in enumerate(ORDER):
        if n:
            inner(n, f)
    for f in ORDER[1:EARLY]:
        for side in range(2):
            halos[f, side].wait_recv()
        outer(f)
    a = Analysis(
        tab_ref, row_ref, count_ref, part_ref, anom_ref, scaled_ref, innov_ref, lhs_ref,
        weight_ref, dev_ref, done_ref,
    )
    for f in ORDER[:EARLY]:
        a.spread_field(0, x_ref, f)
    for f in ORDER[EARLY:]:
        send_rows(f)
    for copy in records:
        copy.wait_recv()
    swap = pltpu.make_async_remote_copy(
        src_ref=got_ref.at[:, :, core],
        dst_ref=got_ref.at[:, :, core],
        send_sem=swap_send,
        recv_sem=swap_recv,
        device_id=sibling,
        device_id_type=MESH,
    )
    swap.start()
    swap.wait_recv()

    slots_ref[...] = got_ref[...].reshape(SLOTS, 128)
    for i, piece in enumerate(split3(slots_ref[...])):
        part_ref[i] = piece
    for j in range(WIDE):
        a.finish(0, j, *a.load(0, j), grid=j == 0)
    tab, prior = a.load(1, 0)
    inside, deviation = a.deviation_of(prior)
    total = sum(a.effect(j, tab, deviation) for j in range(WIDE))
    a.finish(1, 0, tab, inside + prior[:, M : M + 1] * total)
    for f in ORDER[:EARLY]:
        a.apply_field(0, x_ref, f)
    for f in ORDER[:EARLY]:
        a.spread_field(1, done_ref, f)
        a.apply_field(1, done_ref, f)
    for f in ORDER[EARLY:]:
        for side in range(2):
            halos[f, side].wait_recv()
        outer(f)
        a.spread_field(0, x_ref, f)
    for f in ORDER[EARLY:]:
        a.apply_field(0, x_ref, f)
    for f in ORDER[EARLY:]:
        a.spread_field(1, done_ref, f)
        a.apply_field(1, done_ref, f)
    swap.wait_send()
    for copy in records:
        copy.wait_send()
    for f in ORDER:
        for side in range(2):
            halos[f, side].wait_send()
    for part in range(2):
        for side in range(2):
            edges[part, side].wait_send()


def local(
    ensemble,
    courant_x,
    courant_y,
    diffusion,
    mixing,
    growth,
    land_sea,
    obs_cell,
    obs_value,
    observation_variance,
    obs_perturb,
    radius,
):
    vmem = pl.BlockSpec(memory_space=pltpu.VMEM)
    hbm = pl.BlockSpec(memory_space=pltpu.HBM)
    shape = jax.ShapeDtypeStruct
    dma = pltpu.SemaphoreType.DMA
    most = SLOTS // BLOCK
    done, x, slots, tab, rows, count = pl.pallas_call(
        forecast_kernel,
        out_shape=(
            shape((FIELDS * ROWS, M, COLS), F32),
            shape((FIELDS * ROWS, M, COLS), F32),
            shape((SLOTS, 128), F32),
            shape((2, SLOTS, 128), F32),
            shape((2, 8, SLOTS), F32),
            shape((8, 128), F32),
        ),
        in_specs=[hbm] * 11 + [pl.BlockSpec(memory_space=pltpu.SMEM)],
        out_specs=(vmem,) * 6,
        scratch_shapes=[
            pltpu.VMEM((FIELDS, ROWS, M, COLS), F32),
            pltpu.VMEM((FIELDS, 2, 2, M, COLS), F32),
            pltpu.VMEM((FIELDS, 8, 128), F32),
            pltpu.VMEM((2, FIELDS, 8, 128), F32),
            pltpu.VMEM((8, 128), F32),
            pltpu.VMEM((3, TY // 2, 2, CAP, 128), F32),
            pltpu.VMEM((2, CHUNKS, 128), jnp.int32),
            pltpu.VMEM((2, CHUNKS, 128), F32),
            pltpu.VMEM((CHUNKS, 128, 128), F32),
            pltpu.VMEM((8, NOBS), F32),
            pltpu.VMEM((SLOTS, NOBS), BF16),
            pltpu.VMEM((2 * ROWS, 12, 8, 128), F32),
            pltpu.VMEM((2 * ROWS, COLS), F32),
            pltpu.VMEM((2 * ROWS, COLS), F32),
            pltpu.VMEM((ROWS, COLS), F32),
            pltpu.VMEM((ROWS, COLS), F32),
            pltpu.VMEM((2 * ROWS, COLS), F32),
            pltpu.VMEM((ROWS, COLS), jnp.int32),
            pltpu.VMEM((2, NOBS), jnp.int32),
            pltpu.VMEM((2, NOBS), F32),
            pltpu.VMEM((2, NOBS), F32),
            pltpu.VMEM((2, M, NOBS), F32),
            pltpu.VMEM((3, SLOTS, 128), BF16),
            pltpu.VMEM((2, 1, BLOCK, 128), BF16),
            pltpu.VMEM((WIDE, BLOCK, 128), F32),
            pltpu.VMEM((WIDE, BLOCK, 128), F32),
            pltpu.VMEM((2, 1, 2 * M, 2 * BLOCK), BF16),
            pltpu.VMEM((2, 1, BLOCK, ROWS * COLS), F32),
            pltpu.VMEM((2, FIELDS, 128, ROWS * COLS), BF16),
            dma((10,)),
            dma((FIELDS, ROWS)),
            dma((FIELDS, 2)),
            dma((FIELDS, 2)),
            dma((2, 2)),
            dma((2, 2)),
            dma((len(PARTNERS),)),
            dma((len(PARTNERS),)),
            dma,
            dma,
        ],
        compiler_params=pltpu.CompilerParams(
            collective_id=0, has_side_effects=True, vmem_limit_bytes=40 << 20
        ),
    )(
        *(
            pltpu.with_memory_space_constraint(array, pltpu.HBM)
            for array in (
                ensemble.reshape(M, FIELDS * ROWS, 1, COLS),
                courant_x.reshape(2 * ROWS, COLS),
                courant_y.reshape(2 * ROWS, COLS),
                diffusion,
                mixing,
                growth.reshape(2 * ROWS, COLS),
                land_sea,
                obs_cell,
                obs_value,
                observation_variance,
                jnp.swapaxes(obs_perturb, 1, 2),
            )
        ),
        radius,
    )
    out = pl.pallas_call(
        analysis_kernel,
        out_shape=shape((M, FIELDS * ROWS, 1, COLS), F32),
        in_specs=[vmem] * 6,
        out_specs=hbm,
        scratch_shapes=[
            pltpu.VMEM((3, SLOTS, 128), BF16),
            pltpu.VMEM((2, most, BLOCK, 128), BF16),
            pltpu.VMEM((most, BLOCK, 128), F32),
            pltpu.VMEM((most, BLOCK, 128), F32),
            pltpu.VMEM((2, most, 2 * M, 2 * BLOCK), BF16),
            pltpu.VMEM((2, most, BLOCK, ROWS * COLS), F32),
            pltpu.VMEM((2, FIELDS, 128, ROWS * COLS), BF16),
            pltpu.VMEM((FIELDS * ROWS, M, COLS), F32),
            dma((FIELDS * ROWS,)),
        ],
        compiler_params=pltpu.CompilerParams(vmem_limit_bytes=40 << 20),
    )(done, x, slots, tab, rows, count)
    return out.reshape(ensemble.shape)


def solution(mesh):
    placed = (
        P(None, None, "gy", "gx"),
        P(None, "gy", "gx"),
        P(None, "gy", "gx"),
        P("gy", "gx"),
        P("gy", "gx"),
        P(None, "gy", "gx"),
        P("gy", "gx"),
        P(),
        P(),
        P(),
        P(),
        P(),
    )
    return jax.shard_map(
        local, mesh=mesh, in_specs=placed, out_specs=P(None, None, "gy", "gx"), check_vma=False
    )
```

```python
import functools

import jax
import jax.numpy as jnp
from jax import lax
from jax.experimental import pallas as pl
from jax.experimental.pallas import tpu as pltpu
from jax.sharding import PartitionSpec as P

MESH = pl.DeviceIdType.MESH
F32 = jnp.float32
BF16 = jnp.bfloat16
M = 40
FIELDS = 8
ROWS = 4
COLS = 128
TX = 32
TY = 16
NX = 4096
NOBS = 1024
CAP = 8
SLOTS = 3 * TY * CAP
CHUNKS = NOBS // 128
BLOCK = 128
WIDE = 2
ORDER = (1, 0, 2, 3, 4, 5, 6, 7)
EARLY = 4
PARTNERS = [
    (dc, dj) for dj in (4, 3, 5, 2, 6, 1, 7, 0) for dc in (1, -1, 0) if (dc, dj) != (0, 0)
]


def dot(a, b):
    return lax.dot_general(a, b, (((1,), (0,)), ((), ())), preferred_element_type=F32)


def dot_t(a, b):
    return lax.dot_general(a, b, (((1,), (1,)), ((), ())), preferred_element_type=F32)


def split3(x):
    high = x.astype(BF16)
    rest = x - high.astype(F32)
    mid = rest.astype(BF16)
    low = (rest - mid.astype(F32)).astype(BF16)
    return high, mid, low


def iota(shape, dim):
    return lax.broadcasted_iota(jnp.int32, shape, dim)


class Analysis:
    def __init__(self, tab, row, count, part, anom, scaled, innov, lhs, weight, dev, state):
        self.tab, self.row, self.part = tab, row, part
        self.anom, self.scaled, self.innov = anom, scaled, innov
        self.lhs, self.weight, self.dev, self.state = lhs, weight, dev, state
        self.gx, self.gy = lax.axis_index("gx"), lax.axis_index("gy")
        self.lane = iota((BLOCK, 128), 1)
        self.member = self.lane < M
        self.per_square = 1.0 / count[3:4, :]
        self.ocean = count[4:8, :]
        self.exact = functools.partial(
            lax.dot_general, precision=lax.Precision.HIGHEST, preferred_element_type=F32
        )

    def near_x(self, gap):
        gap = jnp.where(gap >= NX / 2, gap - NX, gap)
        return jnp.where(gap < -NX / 2, gap + NX, gap)

    def load(self, b, j):
        start = j * BLOCK if isinstance(j, int) else pl.multiple_of(j * BLOCK, BLOCK)
        tab = self.tab[b, pl.ds(start, BLOCK), :]
        slot = tab[:, M + 4 : M + 5]
        hot = jnp.where(iota((BLOCK, SLOTS), 1).astype(F32) == slot, 1.0, 0.0).astype(BF16)
        prior = dot(hot, self.part[0]) + dot(hot, self.part[1]) + dot(hot, self.part[2])
        if b:
            prior = pltpu.roll(prior, 64, 1)
        return tab, prior

    def deviation_of(self, prior):
        inside = jnp.where(self.member, prior, 0.0)
        mean = jnp.sum(inside, axis=1, keepdims=True) * (1.0 / M)
        return inside, jnp.where(self.member, inside - mean, 0.0)

    def finish(self, b, j, tab, prior, grid=True):
        prior, anomaly = self.deviation_of(prior)
        spread = jnp.sum(anomaly * anomaly, axis=1, keepdims=True) * (1.0 / (M - 1))
        filled = tab[:, M + 5 : M + 6]
        scale = filled / ((M - 1) * (spread + tab[:, M + 1 : M + 2] + (1.0 - filled)))
        innovation = jnp.where(self.member, tab, 0.0) - prior
        if b == 0:
            self.scaled[j] = anomaly * scale
            self.innov[j] = innovation
        if not grid:
            return
        high = anomaly.astype(BF16).astype(F32)
        lhs = high + pltpu.roll(high, M, 1) + pltpu.roll(anomaly - high, 2 * M, 1)
        self.anom[b, j] = lhs.astype(BF16)
        turned = innovation.T[0:M, :]
        high = turned.astype(BF16).astype(F32)
        lhs = jnp.concatenate(
            [
                jnp.concatenate([high, high], axis=1),
                jnp.concatenate([turned - high, jnp.zeros_like(high)], axis=1),
            ],
            axis=0,
        )
        self.lhs[b, j] = lhs.astype(BF16)
        gap = self.near_x(tab[:, M + 3 : M + 4] - (self.gx * COLS + self.lane).astype(F32))
        square = gap * gap
        for r in range(ROWS):
            gap = tab[:, M + 2 : M + 3] - (self.gy * ROWS + r).astype(F32)
            taper = jnp.maximum(0.0, 1.0 - (square + gap * gap) * self.per_square)
            self.weight[b, j, :, 128 * r : 128 * r + 128] = taper * scale

    def effect(self, i, tab, deviation):
        cover = self.exact(deviation, self.scaled[i], (((1,), (1,)), ((), ())))
        start = i * BLOCK if isinstance(i, int) else pl.multiple_of(i * BLOCK, BLOCK)
        window = pl.ds(start, BLOCK)
        gap_x = self.near_x(self.row[0, 3:4, window] - tab[:, M + 3 : M + 4])
        gap_y = self.row[0, 2:3, window] - tab[:, M + 2 : M + 3]
        taper = jnp.maximum(0.0, 1.0 - (gap_x * gap_x + gap_y * gap_y) * self.per_square)
        return self.exact(cover * taper, self.innov[i], (((1,), (0,)), ((), ())))

    def spread_field(self, b, source, f):
        for r in range(ROWS):
            x = source[f * ROWS + r]
            deviation = x - jnp.sum(x, axis=0, keepdims=True) * (1.0 / M)
            high = deviation.astype(BF16).astype(F32)
            stack = jnp.concatenate(
                [high, deviation - high, high, jnp.zeros((8, 128), F32)], axis=0
            )
            self.dev[b, f, :, 128 * r : 128 * r + 128] = stack.astype(BF16)

    def increment(self, b, j, f):
        cover = dot(self.anom[b, j], self.dev[b, f])
        gain = cover * self.weight[b, j]
        high = gain.astype(BF16)
        low = (gain - high.astype(F32)).astype(BF16)
        both = dot(self.lhs[b, j], jnp.concatenate([high, low], axis=0))
        return both[0:M] + both[M : 2 * M]

    def apply_field(self, b, source, f):
        change = self.increment(b, 0, f)
        for r in range(ROWS):
            self.state[f * ROWS + r] = (
                source[f * ROWS + r]
                + self.ocean[r : r + 1, :] * change[:, 128 * r : 128 * r + 128]
            )


def analysis_kernel(
    done_ref,
    x_ref,
    slots_ref,
    tab_ref,
    row_ref,
    count_ref,
    out_ref,
    part_ref,
    anom_ref,
    scaled_ref,
    innov_ref,
    lhs_ref,
    weight_ref,
    dev_ref,
    state_ref,
    out_sem,
):
    def stores(source):
        for i in range(FIELDS * ROWS):
            yield pltpu.make_async_copy(source.at[i], out_ref.at[:, i, 0, :], out_sem.at[i])

    for copy in stores(done_ref):
        copy.start()
    counts = [jnp.max(count_ref[i : i + 1, :]).astype(jnp.int32) for i in range(3)]
    blocks0, blocks0_wide, blocks1 = [(n + BLOCK - 1) // BLOCK for n in counts]
    for copy in stores(done_ref):
        copy.wait()

    @pl.when((blocks0 > 1) | (blocks0_wide > WIDE) | (blocks1 > 1))
    def _():
        a = Analysis(
            tab_ref, row_ref, count_ref, part_ref, anom_ref, scaled_ref, innov_ref, lhs_ref,
            weight_ref, dev_ref, state_ref,
        )
        for i, piece in enumerate(split3(slots_ref[...])):
            part_ref[i] = piece

        def first_batch(j, carry):
            a.finish(0, j, *a.load(0, j))
            return carry

        lax.fori_loop(0, blocks0_wide, first_batch, 0)

        def second_batch(j, carry):
            tab, prior = a.load(1, j)
            inside, deviation = a.deviation_of(prior)
            total = lax.fori_loop(
                0,
                blocks0_wide,
                lambda i, total: total + a.effect(i, tab, deviation),
                jnp.zeros((BLOCK, 128), F32),
            )
            a.finish(1, j, tab, inside + prior[:, M : M + 1] * total)
            return carry

        lax.fori_loop(0, blocks1, second_batch, 0)
        state_ref[...] = x_ref[...]
        for b, blocks in ((0, blocks0), (1, blocks1)):

            def spread(f, carry, b=b):
                a.spread_field(b, state_ref, f)
                return carry

            lax.fori_loop(0, FIELDS, spread, 0)

            def block(j, carry, b=b):
                def field(f, inner_carry):
                    change = a.increment(b, j, f)
                    for r in range(ROWS):
                        state_ref[f * ROWS + r] += (
                            a.ocean[r : r + 1, :] * change[:, 128 * r : 128 * r + 128]
                        )
                    return inner_carry

                return lax.fori_loop(0, FIELDS, field, carry)

            lax.fori_loop(0, blocks, block, 0)
        for copy in stores(state_ref):
            copy.start()
        for copy in stores(state_ref):
            copy.wait()


def forecast_kernel(
    ens_ref,
    cx_hbm,
    cy_hbm,
    diff_hbm,
    mix_hbm,
    growth_hbm,
    land_hbm,
    cell_hbm,
    value_hbm,
    var_hbm,
    pert_hbm,
    radius_ref,
    done_ref,
    x_ref,
    slots_ref,
    tab_ref,
    row_ref,
    count_ref,
    y_ref,
    halo_ref,
    edge_ref,
    side_ref,
    rec_ref,
    got_ref,
    cell_s,
    rank_s,
    trans_s,
    v_ref,
    hot_ref,
    coef_ref,
    cx_ref,
    cy_ref,
    diff_ref,
    mix_ref,
    growth_ref,
    land_ref,
    cell_ref,
    value_ref,
    var_ref,
    pert_ref,
    part_ref,
    anom_ref,
    scaled_ref,
    innov_ref,
    lhs_ref,
    weight_ref,
    dev_ref,
    small_sem,
    load_sem,
    halo_send,
    halo_recv,
    edge_send,
    edge_recv,
    rec_send,
    rec_recv,
    swap_send,
    swap_recv,
):
    gx = lax.axis_index("gx")
    gy = lax.axis_index("gy")
    core = lax.rem(gy, 2)
    above = (gx, lax.rem(gy + TY - 1, TY))
    below = (gx, lax.rem(gy + 1, TY))
    left = (lax.rem(gx + TX - 1, TX), gy)
    right = (lax.rem(gx + 1, TX), gy)
    sibling = (gx, gy + 1 - 2 * core)

    def partner(dc, dj):
        return (lax.rem(gx + dc + TX, TX), lax.rem(gy + 2 * dj, TY))

    barrier = pltpu.get_barrier_semaphore()
    for device in [partner(dc, dj) for dc, dj in PARTNERS] + [above, below]:
        pl.semaphore_signal(barrier, inc=1, device_id=device, device_id_type=MESH)

    loads = []
    for f in ORDER:
        for r in range(ROWS):
            copy = pltpu.make_async_copy(
                ens_ref.at[:, f * ROWS + r, 0, :], y_ref.at[f, r], load_sem.at[f, r]
            )
            copy.start()
            loads.append(copy)

    sub = iota((8, 128), 0)
    lane = iota((8, 128), 1)
    smalls = []
    for i, (source, target) in enumerate(
        (
            (land_hbm, land_ref),
            (cx_hbm, cx_ref),
            (cy_hbm, cy_ref),
            (diff_hbm, diff_ref),
            (mix_hbm, mix_ref),
            (growth_hbm, growth_ref),
            (cell_hbm, cell_ref),
            (value_hbm, value_ref),
            (var_hbm, var_ref),
            (pert_hbm, pert_ref),
        )
    ):
        copy = pltpu.make_async_copy(source, target, small_sem.at[i])
        copy.start()
        smalls.append(copy)

    for n, f in enumerate(ORDER):
        for r in range(ROWS):
            loads[n * ROWS + r].wait()
        packed = jnp.zeros((8, 128), F32)
        for r in range(ROWS):
            for i in range(M // 8):
                at = 4 * (r * (M // 8) + i)
                moved = pltpu.roll(y_ref[f, r, 8 * i : 8 * i + 8, :], (at + 2) % 128, 1)
                packed = jnp.where((lane >= at) & (lane < at + 4), moved, packed)
        edge_ref[n] = packed

    pl.semaphore_wait(barrier, len(PARTNERS) + 2)

    halos = {}

    def send_rows(f):
        for side, (device, start) in enumerate(((below, 2), (above, 0))):
            copy = pltpu.make_async_remote_copy(
                src_ref=y_ref.at[f, pl.ds(start, 2)],
                dst_ref=halo_ref.at[f, side],
                send_sem=halo_send.at[f, side],
                recv_sem=halo_recv.at[f, side],
                device_id=device,
                device_id_type=MESH,
            )
            copy.start()
            halos[f, side] = copy

    edges = {}

    def send_edges(part, window):
        for side, device in enumerate((right, left)):
            copy = pltpu.make_async_remote_copy(
                src_ref=edge_ref.at[window],
                dst_ref=side_ref.at[side, window],
                send_sem=edge_send.at[part, side],
                recv_sem=edge_recv.at[part, side],
                device_id=device,
                device_id_type=MESH,
            )
            copy.start()
            edges[part, side] = copy

    send_rows(ORDER[0])
    send_edges(0, pl.ds(0, 1))
    send_edges(1, pl.ds(1, FIELDS - 1))
    for f in ORDER[1:EARLY]:
        send_rows(f)

    for copy in smalls:
        copy.wait()

    ocean = land_ref[...].astype(F32)
    first = gy == 0
    last = gy == TY - 1
    for level in range(2):
        for r in range(ROWS):
            at = level * ROWS + r
            o = ocean[r : r + 1, :]
            d = diff_ref[r : r + 1, :] * o
            cx = cx_ref[at : at + 1, :] * o
            cy = cy_ref[at : at + 1, :] * o
            xp, xn = jnp.maximum(cx, 0.0), jnp.minimum(cx, 0.0)
            yp, yn = jnp.maximum(cy, 0.0), jnp.minimum(cy, 0.0)
            terms = [
                1.0 + 0.5 * (xn - xp + yn - yp) - 4.0 * d,
                xn / 6.0,
                d - xp / 3.0 - xn,
                d + xp + xn / 3.0,
                -xp / 6.0,
                yn / 6.0,
                d - yp / 3.0 - yn,
                d + yp + yn / 3.0,
                -yp / 6.0,
            ]
            if r == 0:
                terms[7] = jnp.where(first, 0.0, terms[7])
            if r <= 1:
                terms[8] = jnp.where(first, 0.0, terms[8])
            if r == 3:
                terms[6] = jnp.where(last, 0.0, terms[6])
            if r >= 2:
                terms[5] = jnp.where(last, 0.0, terms[5])
            for i, term in enumerate(terms):
                coef_ref[at, i] = jnp.broadcast_to(term, (8, 128))
            coef_ref[at, 9] = jnp.broadcast_to(o * mix_ref[r : r + 1, :], (8, 128))
            coef_ref[at, 10] = jnp.broadcast_to(o, (8, 128))
            coef_ref[at, 11] = jnp.broadcast_to(growth_ref[at : at + 1, :], (8, 128))

    col_start = gx * COLS
    row_start = gy * ROWS
    me = gx * TY + gy
    big_sub = iota((128, 128), 0)
    big_lane = iota((128, 128), 1)
    own_hot = []
    places = []
    for b in range(2):
        for j in range(CHUNKS):
            cell_s[b, j : j + 1, :] = cell_ref[b : b + 1, 128 * j : 128 * j + 128]
        cell = cell_s[b]
        row = cell >> 12
        col = cell & (NX - 1)
        tile_col = col >> 7
        owner = (tile_col * TY + (row >> 2)).astype(F32)
        for i in range(CHUNKS):
            trans_s[i] = jnp.broadcast_to(owner[i : i + 1, :], (128, 128)).T
        for j in range(CHUNKS):
            mine = jnp.broadcast_to(owner[j : j + 1, :], (128, 128))
            total = jnp.where((trans_s[j] == mine) & (big_sub < big_lane), 1.0, 0.0)
            for i in range(j):
                total = total + jnp.where(trans_s[i] == mine, 1.0, 0.0)
            rank_s[b, j : j + 1, :] = jnp.sum(total, axis=0, keepdims=True)
        rank = rank_s[b]
        own_slot = jnp.where(owner == me.astype(F32), rank, -1.0)
        local_cell = ((row - row_start) * COLS + (col - col_start)).astype(F32)
        subf = sub.astype(F32)
        spot = jnp.zeros((8, 128), F32)
        fill = jnp.zeros((8, 128), F32)
        for j in range(CHUNKS):
            hit = subf == own_slot[j : j + 1, :]
            spot = spot + jnp.where(hit, local_cell[j : j + 1, :], 0.0)
            fill = fill + jnp.where(hit, 1.0, 0.0)
        spot = jnp.sum(spot, axis=1, keepdims=True)
        fill = jnp.sum(fill, axis=1, keepdims=True)
        lane512 = iota((8, ROWS * COLS), 1).astype(F32)
        own_hot.append(jnp.where((spot == lane512) & (fill > 0.0), 1.0, 0.0))
        places.append((row, col, tile_col, rank))
    own_hot = jnp.concatenate(own_hot, axis=0).astype(BF16)

    reach = radius_ref[0] * radius_ref[0]
    upper = jnp.where(big_sub < big_lane, 1.0, 0.0).astype(BF16)

    def before(flag):
        flag = jnp.where(flag, 1.0, 0.0)
        inside = dot(flag.astype(BF16), upper)
        own = jnp.broadcast_to(jnp.sum(flag, axis=1, keepdims=True), (8, 128))
        run = own
        for step in (1, 2, 4):
            run = run + jnp.where(sub >= step, pltpu.roll(run, step, 0), 0.0)
        return inside + run - own, run[7:8, :]

    count_ref[3:4, :] = jnp.full((1, 128), reach, jnp.int32).astype(F32)
    count_ref[4:8, :] = ocean
    for b in range(2):
        row, col, tile_col, rank = places[b]
        relative = (tile_col - gx + 33) & (TX - 1)
        slot = ((relative * TY + (row >> 2)) * CAP).astype(F32) + rank
        offset = ((col - (col_start + 64) + 2048 + NX) & (NX - 1)) - 2048
        gap_x = jnp.maximum(0, jnp.maximum(offset - 63, -64 - offset))
        gap_y = jnp.maximum(0, jnp.maximum(row - (row_start + 3), row_start - row))
        gap = gap_x * gap_x + gap_y * gap_y
        near = gap < reach
        place, count = before(near)
        place = jnp.where(near, place, -1.0)
        count_ref[2 * b : 2 * b + 1, :] = count
        if b == 0:
            beyond = (gap >= reach) & (gap < 4 * reach)
            place2, count2 = before(beyond)
            place = jnp.where(beyond, place2 + count, place)
            count_ref[1:2, :] = count + count2
        v_ref[0:1, :] = value_ref[b : b + 1, :]
        v_ref[1:2, :] = var_ref[b : b + 1, :]
        rowf, colf = row.astype(F32), col.astype(F32)
        for j in range(CHUNKS):
            window = slice(128 * j, 128 * j + 128)
            v_ref[2:3, window] = rowf[j : j + 1, :]
            v_ref[3:4, window] = colf[j : j + 1, :]
            v_ref[4:5, window] = slot[j : j + 1, :]
        v_ref[5:8, :] = jnp.ones((3, NOBS), F32)
        index = iota((SLOTS, 128), 0).astype(F32)
        for j in range(CHUNKS):
            hot = jnp.where(index == place[j : j + 1, :], 1.0, 0.0)
            hot_ref[:, 128 * j : 128 * j + 128] = hot.astype(BF16)
        hot = hot_ref[...]
        vs = split3(v_ref[...])
        column = dot_t(hot, vs[0]) + dot_t(hot, vs[1]) + dot_t(hot, vs[2])
        row_ref[b] = dot_t(vs[0], hot) + dot_t(vs[1], hot) + dot_t(vs[2], hot)
        ps = split3(pert_ref[b])
        noise = dot_t(hot, ps[0]) + dot_t(hot, ps[1]) + dot_t(hot, ps[2])
        tab_ref[b] = jnp.zeros((SLOTS, 128), F32)
        tab_ref[b, :, 0:M] = column[:, 0:1] + jnp.sqrt(column[:, 1:2]) * noise
        tab_ref[b, :, M : M + 8] = column

    def by_member(value, r, at):
        return jnp.broadcast_to(coef_ref[at, value][None], (M // 8, 8, 128)).reshape(M, 128)

    wide_lane = iota((M, 128), 1)

    def inner(n, f):
        level, tracer = divmod(f, 4)
        base = level * 4
        merged = jnp.where((lane & 3) < 2, side_ref[0, n], side_ref[1, n])
        for r in range(ROWS):
            at = level * ROWS + r
            c = functools.partial(by_member, r=r, at=at)
            q = y_ref[f, r]
            halo = jnp.concatenate(
                [
                    pltpu.roll(merged, (126 - 4 * (r * (M // 8) + i)) % 128, 1)
                    for i in range(M // 8)
                ],
                axis=0,
            )
            total = q * c(0)
            total += c(1) * pltpu.roll(jnp.where(wide_lane < 2, halo, q), 126, 1)
            total += c(2) * pltpu.roll(jnp.where(wide_lane < 1, halo, q), 127, 1)
            total += c(3) * pltpu.roll(jnp.where(wide_lane > 126, halo, q), 1, 1)
            total += c(4) * pltpu.roll(jnp.where(wide_lane > 125, halo, q), 2, 1)
            for value, shift in ((5, 2), (6, 1), (7, -1), (8, -2)):
                if 0 <= r + shift < ROWS:
                    total += c(value) * y_ref[f, r + shift]
            total += c(9) * (y_ref[(1 - level) * 4 + tracer, r] - q)
            plankton = y_ref[base + 1, r]
            grazer = y_ref[base + 2, r]
            uptake = grazing = 0.0
            if tracer in (0, 1):
                nutrient = jnp.abs(y_ref[base, r])
                uptake = c(11) * nutrient / (nutrient + 0.5) * plankton
            if tracer in (1, 2, 3):
                size = jnp.abs(plankton)
                grazing = 0.3 * grazer * size / (size + 0.5)
            if tracer == 0:
                change = 0.1 * y_ref[base + 3, r] - uptake
            elif tracer == 1:
                change = uptake - grazing - 0.05 * plankton
            elif tracer == 2:
                change = 0.3 * grazing - 0.05 * grazer
            else:
                change = 0.7 * grazing + 0.05 * plankton + 0.05 * grazer - 0.1 * q
            x_ref[f * ROWS + r] = total + c(10) * change

    def outer(f):
        at = f // 4 * ROWS
        far, near = halo_ref[f, 0, 0], halo_ref[f, 0, 1]
        x_ref[f * ROWS] += by_member(8, 0, at) * far + by_member(7, 0, at) * near
        x_ref[f * ROWS + 1] += by_member(8, 1, at + 1) * near
        near, far = halo_ref[f, 1, 0], halo_ref[f, 1, 1]
        x_ref[f * ROWS + 2] += by_member(5, 2, at + 2) * near
        x_ref[f * ROWS + 3] += by_member(5, 3, at + 3) * far + by_member(6, 3, at + 3) * near

    f = ORDER[0]
    for side in range(2):
        edges[0, side].wait_recv()
    inner(0, f)
    for side in range(2):
        halos[f, side].wait_recv()
    outer(f)

    fields = jnp.concatenate(
        [
            jnp.concatenate(
                [x_ref[f * ROWS + r], jnp.broadcast_to(ocean[r : r + 1, :], (8, 128))], axis=0
            )
            for r in range(ROWS)
        ],
        axis=1,
    )
    high, mid, low = split3(fields)
    prior = dot_t(own_hot, high) + dot_t(own_hot, mid) + dot_t(own_hot, low)
    rec_ref[...] = jnp.zeros((8, 128), F32)
    rec_ref[:, 0:48] = prior[0:8]
    rec_ref[:, 64:112] = prior[8:16]
    half = gy // 2
    got_ref[1, half, core] = rec_ref[...]
    records = []
    for i, (dc, dj) in enumerate(PARTNERS):
        copy = pltpu.make_async_remote_copy(
            src_ref=rec_ref,
            dst_ref=got_ref.at[1 - dc, half, core],
            send_sem=rec_send.at[i],
            recv_sem=rec_recv.at[i],
            device_id=partner(dc, dj),
            device_id_type=MESH,
        )
        copy.start()
        records.append(copy)

    for side in range(2):
        edges[1, side].wait_recv()
    for n, f in enumerate(ORDER):
        if n:
            inner(n, f)
    for f in ORDER[1:EARLY]:
        for side in range(2):
            halos[f, side].wait_recv()
        outer(f)
    a = Analysis(
        tab_ref, row_ref, count_ref, part_ref, anom_ref, scaled_ref, innov_ref, lhs_ref,
        weight_ref, dev_ref, done_ref,
    )
    for f in ORDER[:EARLY]:
        a.spread_field(0, x_ref, f)
    for f in ORDER[EARLY:]:
        send_rows(f)
    for copy in records:
        copy.wait_recv()
    swap = pltpu.make_async_remote_copy(
        src_ref=got_ref.at[:, :, core],
        dst_ref=got_ref.at[:, :, core],
        send_sem=swap_send,
        recv_sem=swap_recv,
        device_id=sibling,
        device_id_type=MESH,
    )
    swap.start()
    swap.wait_recv()

    slots_ref[...] = got_ref[...].reshape(SLOTS, 128)
    for i, piece in enumerate(split3(slots_ref[...])):
        part_ref[i] = piece
    for j in range(WIDE):
        a.finish(0, j, *a.load(0, j), grid=j == 0)
    for f in ORDER[:EARLY]:
        a.apply_field(0, x_ref, f)
    tab, prior = a.load(1, 0)
    inside, deviation = a.deviation_of(prior)
    total = sum(a.effect(j, tab, deviation) for j in range(WIDE))
    a.finish(1, 0, tab, inside + prior[:, M : M + 1] * total)
    for f in ORDER[:EARLY]:
        a.spread_field(1, done_ref, f)
        a.apply_field(1, done_ref, f)
    for f in ORDER[EARLY:]:
        for side in range(2):
            halos[f, side].wait_recv()
        outer(f)
        a.spread_field(0, x_ref, f)
    for f in ORDER[EARLY:]:
        a.apply_field(0, x_ref, f)
    for f in ORDER[EARLY:]:
        a.spread_field(1, done_ref, f)
        a.apply_field(1, done_ref, f)
    swap.wait_send()
    for copy in records:
        copy.wait_send()
    for f in ORDER:
        for side in range(2):
            halos[f, side].wait_send()
    for part in range(2):
        for side in range(2):
            edges[part, side].wait_send()


def local(
    ensemble,
    courant_x,
    courant_y,
    diffusion,
    mixing,
    growth,
    land_sea,
    obs_cell,
    obs_value,
    observation_variance,
    obs_perturb,
    radius,
):
    vmem = pl.BlockSpec(memory_space=pltpu.VMEM)
    hbm = pl.BlockSpec(memory_space=pltpu.HBM)
    shape = jax.ShapeDtypeStruct
    dma = pltpu.SemaphoreType.DMA
    most = SLOTS // BLOCK
    done, x, slots, tab, rows, count = pl.pallas_call(
        forecast_kernel,
        out_shape=(
            shape((FIELDS * ROWS, M, COLS), F32),
            shape((FIELDS * ROWS, M, COLS), F32),
            shape((SLOTS, 128), F32),
            shape((2, SLOTS, 128), F32),
            shape((2, 8, SLOTS), F32),
            shape((8, 128), F32),
        ),
        in_specs=[hbm] * 11 + [pl.BlockSpec(memory_space=pltpu.SMEM)],
        out_specs=(vmem,) * 6,
        scratch_shapes=[
            pltpu.VMEM((FIELDS, ROWS, M, COLS), F32),
            pltpu.VMEM((FIELDS, 2, 2, M, COLS), F32),
            pltpu.VMEM((FIELDS, 8, 128), F32),
            pltpu.VMEM((2, FIELDS, 8, 128), F32),
            pltpu.VMEM((8, 128), F32),
            pltpu.VMEM((3, TY // 2, 2, CAP, 128), F32),
            pltpu.VMEM((2, CHUNKS, 128), jnp.int32),
            pltpu.VMEM((2, CHUNKS, 128), F32),
            pltpu.VMEM((CHUNKS, 128, 128), F32),
            pltpu.VMEM((8, NOBS), F32),
            pltpu.VMEM((SLOTS, NOBS), BF16),
            pltpu.VMEM((2 * ROWS, 12, 8, 128), F32),
            pltpu.VMEM((2 * ROWS, COLS), F32),
            pltpu.VMEM((2 * ROWS, COLS), F32),
            pltpu.VMEM((ROWS, COLS), F32),
            pltpu.VMEM((ROWS, COLS), F32),
            pltpu.VMEM((2 * ROWS, COLS), F32),
            pltpu.VMEM((ROWS, COLS), jnp.int32),
            pltpu.VMEM((2, NOBS), jnp.int32),
            pltpu.VMEM((2, NOBS), F32),
            pltpu.VMEM((2, NOBS), F32),
            pltpu.VMEM((2, M, NOBS), F32),
            pltpu.VMEM((3, SLOTS, 128), BF16),
            pltpu.VMEM((2, 1, BLOCK, 128), BF16),
            pltpu.VMEM((WIDE, BLOCK, 128), F32),
            pltpu.VMEM((WIDE, BLOCK, 128), F32),
            pltpu.VMEM((2, 1, 2 * M, 2 * BLOCK), BF16),
            pltpu.VMEM((2, 1, BLOCK, ROWS * COLS), F32),
            pltpu.VMEM((2, FIELDS, 128, ROWS * COLS), BF16),
            dma((10,)),
            dma((FIELDS, ROWS)),
            dma((FIELDS, 2)),
            dma((FIELDS, 2)),
            dma((2, 2)),
            dma((2, 2)),
            dma((len(PARTNERS),)),
            dma((len(PARTNERS),)),
            dma,
            dma,
        ],
        compiler_params=pltpu.CompilerParams(
            collective_id=0, has_side_effects=True, vmem_limit_bytes=40 << 20
        ),
    )(
        *(
            pltpu.with_memory_space_constraint(array, pltpu.HBM)
            for array in (
                ensemble.reshape(M, FIELDS * ROWS, 1, COLS),
                courant_x.reshape(2 * ROWS, COLS),
                courant_y.reshape(2 * ROWS, COLS),
                diffusion,
                mixing,
                growth.reshape(2 * ROWS, COLS),
                land_sea,
                obs_cell,
                obs_value,
                observation_variance,
                jnp.swapaxes(obs_perturb, 1, 2),
            )
        ),
        radius,
    )
    out = pl.pallas_call(
        analysis_kernel,
        out_shape=shape((M, FIELDS * ROWS, 1, COLS), F32),
        in_specs=[vmem] * 6,
        out_specs=hbm,
        scratch_shapes=[
            pltpu.VMEM((3, SLOTS, 128), BF16),
            pltpu.VMEM((2, most, BLOCK, 128), BF16),
            pltpu.VMEM((most, BLOCK, 128), F32),
            pltpu.VMEM((most, BLOCK, 128), F32),
            pltpu.VMEM((2, most, 2 * M, 2 * BLOCK), BF16),
            pltpu.VMEM((2, most, BLOCK, ROWS * COLS), F32),
            pltpu.VMEM((2, FIELDS, 128, ROWS * COLS), BF16),
            pltpu.VMEM((FIELDS * ROWS, M, COLS), F32),
            dma((FIELDS * ROWS,)),
        ],
        compiler_params=pltpu.CompilerParams(vmem_limit_bytes=40 << 20),
    )(done, x, slots, tab, rows, count)
    return out.reshape(ensemble.shape)


def solution(mesh):
    placed = (
        P(None, None, "gy", "gx"),
        P(None, "gy", "gx"),
        P(None, "gy", "gx"),
        P("gy", "gx"),
        P("gy", "gx"),
        P(None, "gy", "gx"),
        P("gy", "gx"),
        P(),
        P(),
        P(),
        P(),
        P(),
    )
    return jax.shard_map(
        local, mesh=mesh, in_specs=placed, out_specs=P(None, None, "gy", "gx"), check_vma=False
    )
```
